128 devices in a mesh: ctx: 16 (over z, x), head: 8 (over y, core).
Axes of the slice: x: 4, y: 4, z: 4, core: 2. Of those that a mesh axis runs over, the one named last changes fastest.
Arguments:
- signal: bfloat16 [16384, 8192], P('ctx', 'head'), may hold values from -6 to 6
- step_size: float32 [128, 16384], P('head', 'ctx'), may hold values from 0.005 to 0.05
- log_decay: float32 [128, 16384], P('head', 'ctx'), may hold values from -0.7 to 0, as said below
- input_map: bfloat16 [16384, 1024], P('ctx', 'head'), may hold values from -1.75 to 1.75
- output_map: bfloat16 [16384, 1024], P('ctx', 'head'), may hold values from -1.75 to 1.75
- skip_gain: float32 [128], P('head'), may hold values from 0.5 to 2
- grad_out: bfloat16 [16384, 8192], P('ctx', 'head'), may hold values from -18 to 18
Outputs:
- grad_signal: bfloat16 [16384, 8192], P('ctx', 'head')
- grad_step: float32 [128, 16384], P('head', 'ctx')
- grad_decay: float32 [128, 16384], P('head', 'ctx')
- grad_input_map: bfloat16 [16384, 1024], P('ctx', 'head')
- grad_output_map: bfloat16 [16384, 1024], P('ctx', 'head')
- grad_skip: float32 [128], P('head')
The draws below stay inside these ranges and needn't reach their ends.
Inputs may be any that keep to these rules, and one draw needn't show every extreme that they name: `log_decay`: log-decays of the state, never positive.
All inputs are finite; a program needn't handle non-finite values.
Results may differ from the reference program's by a relative error of at most 0.001.
Values sent between devices are 32-bit elements; how exact they have to be, the bound alone decides.
No kernel may reach another device: no remote copies, remote signals or barrier semaphores. Data moves between devices by JAX's collectives and lax.ppermute only.
A program may use at most 192 MiB of HBM per device.

```python
import math
import jax
import jax.numpy as jnp
from jax import lax

SSM_HEAD_TOTAL = 128
P_SIZE = 64
N = 128
G = 8
BLOCK = 256
TOK_DEV = 1024
SEQUENCE_SPAN = 16384


def draw_log_decay(key, part):
    parallel_tracks = jax.random.split(key, 7)
    share = 0.5
    slow_heads = jax.random.uniform(parallel_tracks[0], (SSM_HEAD_TOTAL, 1), jnp.float32) < share
    slow_rate = jnp.exp(jax.random.uniform(parallel_tracks[1], (SSM_HEAD_TOTAL, 1), jnp.float32, math.log(0.1), math.log(0.6))) / SEQUENCE_SPAN
    fast_rate = jnp.exp(jax.random.uniform(parallel_tracks[2], (SSM_HEAD_TOTAL, 1), jnp.float32, math.log(1.0 / 50.0), math.log(1.0 / 30.0)))
    rough = jnp.exp(jax.random.uniform(parallel_tracks[3], (SSM_HEAD_TOTAL, SEQUENCE_SPAN), jnp.float32, math.log(0.5), math.log(2.0)))
    block_factor = jnp.exp(jax.random.uniform(parallel_tracks[4], (SSM_HEAD_TOTAL, SEQUENCE_SPAN // TOK_DEV), jnp.float32, math.log(0.5), math.log(2.0)))
    block_factor = jnp.repeat(block_factor, TOK_DEV, axis=1)
    starting_index = jnp.where(slow_heads, slow_rate, fast_rate) * rough * block_factor
    batched_clusters = jax.random.uniform(parallel_tracks[5], (SSM_HEAD_TOTAL, SEQUENCE_SPAN), jnp.float32) < 2.0 / SEQUENCE_SPAN
    recurrence_levels = jax.random.uniform(parallel_tracks[6], (SSM_HEAD_TOTAL, SEQUENCE_SPAN), jnp.float32, 0.2, 0.4)
    entry_lines = -starting_index + jnp.where(batched_clusters, jnp.log1p(-recurrence_levels), 0.0)
    return entry_lines.astype(jnp.float32)


def draw_grad_out(key, part):
    positions = jnp.arange(SEQUENCE_SPAN, dtype=jnp.float32)[:, None] / (SEQUENCE_SPAN - 1)
    entry_lines = jnp.clip(jax.random.normal(key, (SEQUENCE_SPAN, SSM_HEAD_TOTAL * P_SIZE), jnp.float32), -6.0, 6.0) * jnp.exp(positions * math.log(3.0))
    return entry_lines.astype(jnp.bfloat16)


def block_scale(stream_key, dims, cuts, smallest, high):
    loudness, own = 1.0, jax.random.fold_in(stream_key, 6)
    for position, shards_of in cuts:
        draws = jnp.exp(jax.random.uniform(jax.random.fold_in(own, position), (shards_of,), jnp.float32, smallest / len(cuts), high / len(cuts)))
        loudness = loudness * jnp.repeat(draws, dims[position] // shards_of).reshape([-1 if axis == position else 1 for axis in range(len(dims))])
    return loudness


def bell_draw(own_key, dims, scale, limit, cuts=(), kind=jnp.bfloat16):
    values = scale * jax.random.normal(own_key, dims, jnp.float32)
    if cuts:
        values = values * block_scale(own_key, dims, cuts, -0.22, 0.18)
    return jnp.clip(values, -limit, limit).astype(kind)


def setup_inputs(seed: int = 0) -> dict:
    splits = jax.random.split(jax.random.key(seed), 8)
    signal = bell_draw(splits[0], (SEQUENCE_SPAN, SSM_HEAD_TOTAL * P_SIZE), 1.0, 6.0, ((0, 16), (1, 8)))
    step_size = jnp.clip(jnp.exp(math.log(0.05) - 2.3025851 * jax.random.uniform(splits[1], (SSM_HEAD_TOTAL, SEQUENCE_SPAN), jnp.float32) ** block_scale(splits[1], (SSM_HEAD_TOTAL, SEQUENCE_SPAN), ((0, 8), (1, 16)), -0.2, 0.2)), 0.005, 0.05)
    log_decay = draw_log_decay(jax.random.fold_in(splits[7], 71), 0)
    input_map = bell_draw(splits[3], (SEQUENCE_SPAN, G * N), 0.3, 1.75, ((0, 16), (1, 8)))
    output_map = bell_draw(splits[4], (SEQUENCE_SPAN, G * N), 0.3, 1.75, ((0, 16), (1, 8)))
    skip_gain = jnp.clip(0.5 + 1.5 * jax.random.uniform(splits[5], (SSM_HEAD_TOTAL,), jnp.float32) ** block_scale(splits[5], (SSM_HEAD_TOTAL,), ((0, 8),), -0.2, 0.2), 0.5, 2.0)
    grad_out = draw_grad_out(jax.random.fold_in(splits[7], 71), 0)
    return {"signal": signal, "step_size": step_size, "log_decay": log_decay, "input_map": input_map, "output_map": output_map, "skip_gain": skip_gain, "grad_out": grad_out}


HIGH = lax.Precision.HIGHEST

def block_forward(tokens_in, steps_in, decays_in, keys_in, queries_in, gains_in, block):
    length, groups, heads, width = tokens_in.shape
    entries = keys_in.shape[2]
    number = length // block
    tokens = tokens_in.reshape(number, block, groups, heads, width)
    keys = keys_in.reshape(number, block, groups, entries)
    queries = queries_in.reshape(number, block, groups, entries)
    steps = steps_in.reshape(groups, heads, number, block)
    cumulative = jnp.cumsum(decays_in.reshape(groups, heads, number, block), axis=-1)
    row_ids = lax.broadcasted_iota(jnp.int32, (block, block), 0)
    col_ids = lax.broadcasted_iota(jnp.int32, (block, block), 1)
    lower_mask = row_ids >= col_ids
    spread = cumulative[..., :, None] - cumulative[..., None, :]
    decays = jnp.exp(jnp.where(lower_mask, spread, -jnp.inf))
    scores = jnp.einsum('kqgn,ksgn->gkqs', queries, keys, precision=HIGH)
    weights = decays * scores[:, None] * steps[..., None, :]
    inner = jnp.einsum('ghkqs,ksghp->kqghp', weights, tokens, precision=HIGH)
    tails = jnp.exp(cumulative[..., -1:] - cumulative) * steps
    scaled = tokens * jnp.transpose(tails, (2, 3, 0, 1))[..., None]
    states = jnp.einsum('ksghp,ksgn->kghpn', scaled, keys, precision=HIGH)
    totals = jnp.moveaxis(cumulative[..., -1], -1, 0)

    def advance(carried, item):
        state_now, total_now = item
        return (jnp.exp(total_now)[..., None, None] * carried + state_now, carried)
    zero_state = jnp.zeros((groups, heads, width, entries), jnp.float32)
    final, entering = lax.scan(advance, zero_state, (states, totals))
    outer = jnp.einsum('kqgn,kghpn->kqghp', queries, entering, precision=HIGH)
    outer = outer * jnp.transpose(jnp.exp(cumulative), (2, 3, 0, 1))[..., None]
    result = inner + outer + gains_in[:, :, None] * tokens
    return (result.reshape(length, groups, heads, width), final)

def reference(signal, step_size, log_decay, input_map, output_map, skip_gain, grad_out):
    per_group = SSM_HEAD_TOTAL // G
    sig_all = jnp.transpose(signal.astype(jnp.float32).reshape(SEQUENCE_SPAN, G, per_group, P_SIZE), (1, 0, 2, 3))
    upstream = jnp.transpose(grad_out.astype(jnp.float32).reshape(SEQUENCE_SPAN, G, per_group, P_SIZE), (1, 0, 2, 3))
    steps_all = step_size.reshape(G, per_group, SEQUENCE_SPAN)
    decays_all = log_decay.reshape(G, per_group, SEQUENCE_SPAN)
    keys_all = jnp.transpose(input_map.astype(jnp.float32).reshape(SEQUENCE_SPAN, G, N), (1, 0, 2))
    queries_all = jnp.transpose(output_map.astype(jnp.float32).reshape(SEQUENCE_SPAN, G, N), (1, 0, 2))
    gains_all = skip_gain.reshape(G, per_group)

    def one_group(item):
        sig_one, step_one, decay_one, key_one, query_one, gain_one, upstream_one = item

        def forward_pass(sig_in, step_in, decay_in, key_in, query_in, gain_in):
            return block_forward(sig_in[:, None], step_in[None], decay_in[None], key_in[:, None], query_in[:, None], gain_in[None], BLOCK)
        outputs, pullback = jax.vjp(forward_pass, sig_one, step_one, decay_one, key_one, query_one, gain_one)
        return pullback((upstream_one[:, None], jnp.zeros_like(outputs[1])))
    grads = lax.map(one_group, (sig_all, steps_all, decays_all, keys_all, queries_all, gains_all, upstream))
    grad_signal = jnp.transpose(grads[0], (1, 0, 2, 3)).reshape(SEQUENCE_SPAN, SSM_HEAD_TOTAL * P_SIZE).astype(jnp.bfloat16)
    grad_step = grads[1].reshape(SSM_HEAD_TOTAL, SEQUENCE_SPAN)
    grad_decay = grads[2].reshape(SSM_HEAD_TOTAL, SEQUENCE_SPAN)
    grad_input_map = jnp.transpose(grads[3], (1, 0, 2)).reshape(SEQUENCE_SPAN, G * N).astype(jnp.bfloat16)
    grad_output_map = jnp.transpose(grads[4], (1, 0, 2)).reshape(SEQUENCE_SPAN, G * N).astype(jnp.bfloat16)
    grad_skip = grads[5].reshape(SSM_HEAD_TOTAL)
    return (grad_signal, grad_step, grad_decay, grad_input_map, grad_output_map, grad_skip)
```

```python
import jax
import jax.numpy as jnp
from jax import lax
from jax.experimental import pallas as pl
from jax.experimental.pallas import tpu as pltpu
from jax.sharding import PartitionSpec as P

P_SIZE = 64
N = 128
HEADS = 16
Q = 128
WIDE = HEADS * P_SIZE
ROWS = N + 8
LOG2E = 1.4426950408889634
NEG = -1e30
HIGH = lax.Precision.HIGHEST
f32 = jnp.float32
bf16 = jnp.bfloat16


def iota(shape, dim):
    return lax.broadcasted_iota(jnp.int32, shape, dim)


def split(z):
    hi = z.astype(bf16)
    lo = (z - hi.astype(f32)).astype(bf16)
    return hi, lo


def dot(a, b, ca, cb, precision=None):
    return lax.dot_general(
        a, b, (((ca,), (cb,)), ((), ())), precision=precision, preferred_element_type=f32
    )


def twice(a, axis):
    return jnp.concatenate([a, a], axis=axis)


def selector():
    return (iota((HEADS, WIDE), 1) // P_SIZE == iota((HEADS, WIDE), 0)).astype(f32).astype(bf16)


def expand(rows, sel2):
    hi, lo = split(rows)
    return dot(jnp.concatenate([hi, lo], axis=0), sel2, 0, 0)


def per_head(z, sel):
    hi, lo = split(z)
    return dot(sel, hi, 1, 1) + dot(sel, lo, 1, 1)


def cumulative(decay):
    upper = (iota((Q, Q), 0) <= iota((Q, Q), 1)).astype(f32)
    return dot(decay * LOG2E, upper, 1, 0, HIGH)


def low_half(shape):
    return iota(shape, len(shape) - 1) < P_SIZE


def own_kernel(x_ref, dy_ref, b_ref, c_ref, dt_ref, a_ref, pay_ref, h_ref, p_ref, run_ref, sk_ref):
    k = pl.program_id(0)

    @pl.when(k == 0)
    def _():
        h_ref[...] = jnp.zeros_like(h_ref)
        p_ref[...] = jnp.zeros_like(p_ref)
        run_ref[...] = jnp.zeros_like(run_ref)
        sk_ref[...] = jnp.zeros_like(sk_ref)

    sel = selector()
    sel2 = twice(sel, 0)
    cum = cumulative(a_ref[...])
    tot = jnp.broadcast_to(cum[:, Q - 1 : Q], (HEADS, Q))
    run = run_ref[...]
    x = x_ref[...].astype(f32)
    dy = dy_ref[...].astype(f32)
    xs = x * expand(jnp.exp2(tot - cum) * dt_ref[...], sel2)
    ds = dy * expand(jnp.exp2(cum + run), sel2)
    fade = expand(jnp.exp2(tot), sel2)
    h_ref[...] = h_ref[...] * fade + dot(
        twice(b_ref[...], 0), jnp.concatenate(split(xs), axis=0), 0, 0
    )
    p_ref[...] = p_ref[...] + dot(
        twice(c_ref[...], 0), jnp.concatenate(split(ds), axis=0), 0, 0
    )
    sk_ref[...] = sk_ref[...] + jnp.sum((x * dy).reshape(Q // 8, 8, WIDE), axis=0)
    run_ref[...] = run + tot

    @pl.when(k == pl.num_programs(0) - 1)
    def _():
        run_end = run_ref[...]
        skip = jnp.sum(dot(sel.astype(f32), sk_ref[...], 1, 1, HIGH), axis=1, keepdims=True)
        skip = jnp.broadcast_to(skip, (HEADS, N))
        low = low_half((N, 128))
        row = iota((8, 128), 0)
        for j in range(HEADS // 2):
            hp = h_ref[:, 128 * j : 128 * (j + 1)]
            pp = p_ref[:, 128 * j : 128 * (j + 1)]
            pay_ref[2 * j, 0:N, :] = jnp.where(low, hp, pltpu.roll(pp, P_SIZE, 1))
            pay_ref[2 * j + 1, 0:N, :] = jnp.where(low, pltpu.roll(hp, P_SIZE, 1), pp)
        for h in range(HEADS):
            tail = jnp.where(row == 0, run_end[h : h + 1, :], 0.0)
            pay_ref[h, N:ROWS, :] = jnp.where(row == 1, skip[h : h + 1, :], tail)


def own_part(signal, grad_out, keys, queries, steps, decays):
    length = signal.shape[0]
    tok = lambda width: pl.BlockSpec((Q, width), lambda k: (k, 0))
    row = pl.BlockSpec((HEADS, Q), lambda k: (0, k))
    return pl.pallas_call(
        own_kernel,
        grid=(length // Q,),
        in_specs=[tok(WIDE), tok(WIDE), tok(N), tok(N), row, row],
        out_specs=pl.BlockSpec((HEADS, ROWS, 128), lambda k: (0, 0, 0)),
        out_shape=jax.ShapeDtypeStruct((HEADS, ROWS, 128), f32),
        scratch_shapes=[
            pltpu.VMEM((N, WIDE), f32),
            pltpu.VMEM((N, WIDE), f32),
            pltpu.VMEM((HEADS, 128), f32),
            pltpu.VMEM((8, WIDE), f32),
        ],
        name="own_part",
    )(signal, grad_out, keys, queries, steps, decays)


def scan_kernel(pay_ref, out_ref):
    count = pay_ref.shape[0]
    low = low_half((N, 128))
    state = jnp.zeros((N, 128), f32)
    skip = jnp.zeros((8, 128), f32)
    for d in range(count):
        out_ref[d, 0:N, :] = state
        tail = pay_ref[d, N:ROWS, :]
        skip = skip + tail
        state = state * jnp.exp2(tail[0:1, :]) + pay_ref[d, 0:N, :]
    state = jnp.zeros((N, 128), f32)
    for d in reversed(range(count)):
        out_ref[d, 0:N, :] = jnp.where(low, out_ref[d, 0:N, :], state)
        out_ref[d, N:ROWS, :] = skip
        tail = pay_ref[d, N:ROWS, :]
        state = state * jnp.exp2(tail[0:1, :]) + pay_ref[d, 0:N, :]


def scan_states(pay):
    return pl.pallas_call(
        scan_kernel, out_shape=jax.ShapeDtypeStruct(pay.shape, f32), name="scan_states"
    )(pay)


def inner_kernel(x_ref, dy_ref, b_ref, c_ref, dt_ref, a_ref, u_ref, db_ref, dc_ref, r_ref):
    cum = cumulative(a_ref[...])
    col = jnp.transpose(cum - jnp.log2(dt_ref[...]))
    keys = b_ref[...]
    queries = c_ref[...]
    scores = dot(keys, queries, 1, 1)
    mask = iota((Q, Q), 0) <= iota((Q, Q), 1)
    low = low_half((Q, 128))
    mixed = jnp.zeros((Q, Q), f32)
    for j in range(HEADS // 2):
        lanes = slice(128 * j, 128 * (j + 1))
        dyp = dy_ref[:, lanes]
        zero = jnp.zeros_like(dyp)
        pair = jnp.concatenate([jnp.where(low, dyp, zero), jnp.where(low, zero, dyp)], axis=0)
        gram = dot(x_ref[:, lanes], pair, 1, 1)
        his, los = [], []
        for e in range(2):
            h = 2 * j + e
            g = gram[:, Q * e : Q * (e + 1)]
            decay = jnp.exp2(jnp.where(mask, cum[h : h + 1, :] - col[:, h : h + 1], NEG))
            weights = decay * scores
            mixed = mixed + decay * g
            r_ref[h : h + 1, :] = jnp.sum(weights * g, axis=0, keepdims=True)
            hi, lo = split(weights)
            his.append(hi)
            los.append(lo)
        both = jnp.concatenate(
            [jnp.concatenate(his, axis=1), jnp.concatenate(los, axis=1)], axis=0
        )
        out = dot(both, pair, 1, 0)
        u_ref[:, lanes] = out[:Q] + out[Q:]
    parts = jnp.concatenate(split(mixed), axis=0)
    db = dot(parts, queries, 1, 0)
    db_ref[...] = db[:Q] + db[Q:]
    dc_ref[...] = dot(parts, twice(keys, 0), 0, 0)


def inner_part(signal, grad_out, keys, queries, steps, decays):
    length = signal.shape[0]
    tok = lambda width: pl.BlockSpec((Q, width), lambda k: (k, 0))
    row = pl.BlockSpec((HEADS, Q), lambda k: (0, k))
    return pl.pallas_call(
        inner_kernel,
        grid=(length // Q,),
        in_specs=[tok(WIDE), tok(WIDE), tok(N), tok(N), row, row],
        out_specs=[tok(WIDE), tok(N), tok(N), row],
        out_shape=[
            jax.ShapeDtypeStruct((length, WIDE), f32),
            jax.ShapeDtypeStruct((length, N), f32),
            jax.ShapeDtypeStruct((length, N), f32),
            jax.ShapeDtypeStruct((HEADS, length), f32),
        ],
        name="inner_part",
    )(signal, grad_out, keys, queries, steps, decays)


def outer_kernel(
    x_ref, dy_ref, b_ref, c_ref, dt_ref, a_ref, gain_ref, pay_ref, u_ref, dbi_ref, dci_ref, ri_ref,
    gs_ref, gt_ref, ga_ref, gb_ref, gc_ref, gk_ref, h_ref, g_ref, m_ref,
):
    count = x_ref.shape[0] // Q
    sel = selector()
    sel2 = twice(sel, 0)
    low = low_half((N, 128))
    for j in range(HEADS // 2):
        lanes = slice(128 * j, 128 * (j + 1))
        one = pay_ref[2 * j, 0:N, :]
        two = pay_ref[2 * j + 1, 0:N, :]
        h_ref[:, lanes] = jnp.where(low, one, pltpu.roll(two, P_SIZE, 1))
        g_ref[:, lanes] = jnp.where(low, pltpu.roll(one, P_SIZE, 1), two)
    m_ref[...] = g_ref[...]
    eye = iota((HEADS, 128), 0) == iota((HEADS, 128), 1)
    sums = jnp.zeros((HEADS, 128), f32)
    for h in range(HEADS):
        sums = jnp.where(iota((HEADS, 128), 0) == h, pay_ref[h, N + 1 : N + 2, :], sums)
    gk_ref[...] = jnp.sum(jnp.where(eye, sums, 0.0), axis=0, keepdims=True)[:, :HEADS]
    eye16 = iota((HEADS, HEADS), 0) == iota((HEADS, HEADS), 1)
    gains = jnp.sum(
        jnp.where(eye16, jnp.broadcast_to(gain_ref[...], (HEADS, HEADS)), 0.0),
        axis=1,
        keepdims=True,
    )
    gains = expand(jnp.broadcast_to(gains, (HEADS, Q)), sel2)

    def scales(rows):
        cum = cumulative(a_ref[:, rows])
        tot = jnp.broadcast_to(cum[:, Q - 1 : Q], (HEADS, Q))
        tails = jnp.exp2(tot - cum) * dt_ref[:, rows]
        return expand(tails, sel2), expand(jnp.exp2(cum), sel2), expand(jnp.exp2(tot), sel2)

    def outer_product(hi, lo, other_hi, other_lo):
        first = dot(jnp.concatenate([hi, lo], axis=0), other_hi, 1, 1)
        return first[:Q] + first[Q:] + dot(hi, other_lo, 1, 1)

    for i in range(count):
        rows = slice(Q * i, Q * (i + 1))
        tails, expo, fade = scales(rows)
        keys = b_ref[rows, :]
        queries = c_ref[rows, :]
        state = h_ref[...]
        s_hi, s_lo = split(state)
        dy = dy_ref[rows, :].astype(f32) * expo
        d_hi, d_lo = split(dy)
        out = dot(twice(queries, 1), jnp.concatenate([s_hi, s_lo], axis=0), 1, 0)
        ri_sum = ri_ref[:, rows] + per_head(dy * out, sel)
        ga_ref[:, rows] = ri_sum
        gc_ref[rows, :] = (dci_ref[rows, :] + outer_product(d_hi, d_lo, s_hi, s_lo)).astype(bf16)
        xs = x_ref[rows, :].astype(f32) * tails
        h_ref[...] = state * fade + dot(
            twice(keys, 0), jnp.concatenate(split(xs), axis=0), 0, 0
        )

    for i in reversed(range(count)):
        rows = slice(Q * i, Q * (i + 1))
        tails, expo, fade = scales(rows)
        keys = b_ref[rows, :]
        queries = c_ref[rows, :]
        state = g_ref[...]
        s_hi, s_lo = split(state)
        x = x_ref[rows, :].astype(f32)
        dy = dy_ref[rows, :].astype(f32)
        xs_hi, xs_lo = split(x * tails)
        out = dot(twice(keys, 1), jnp.concatenate([s_hi, s_lo], axis=0), 1, 0)
        u = u_ref[rows, :] + tails * out
        gs_ref[rows, :] = (u + gains * dy).astype(bf16)
        cols = per_head(x * u, sel)
        gt_ref[:, rows] = cols / dt_ref[:, rows]
        ga_ref[:, rows] = ga_ref[:, rows] - cols
        gb_ref[rows, :] = (dbi_ref[rows, :] + outer_product(xs_hi, xs_lo, s_hi, s_lo)).astype(bf16)
        g_ref[...] = state * fade + dot(
            twice(queries, 0), jnp.concatenate(split(dy * expo), axis=0), 0, 0
        )

    ends = jnp.sum((h_ref[...] * m_ref[...]).reshape(N // 8, 8, WIDE), axis=0)
    later = jnp.sum(dot(sel.astype(f32), ends, 1, 1, HIGH), axis=1, keepdims=True)
    lower = (iota((Q, Q), 0) >= iota((Q, Q), 1)).astype(f32)
    for i in reversed(range(count)):
        rows = slice(Q * i, Q * (i + 1))
        after = dot(ga_ref[:, rows], lower, 1, 0, HIGH) + later
        ga_ref[:, rows] = after
        later = after[:, 0:1]


def outer_part(signal, grad_out, keys, queries, steps, decays, gains, pay, inner):
    length = signal.shape[0]
    return pl.pallas_call(
        outer_kernel,
        out_shape=[
            jax.ShapeDtypeStruct((length, WIDE), bf16),
            jax.ShapeDtypeStruct((HEADS, length), f32),
            jax.ShapeDtypeStruct((HEADS, length), f32),
            jax.ShapeDtypeStruct((length, N), bf16),
            jax.ShapeDtypeStruct((length, N), bf16),
            jax.ShapeDtypeStruct((1, HEADS), f32),
        ],
        scratch_shapes=[
            pltpu.VMEM((N, WIDE), f32),
            pltpu.VMEM((N, WIDE), f32),
            pltpu.VMEM((N, WIDE), f32),
        ],
        name="outer_part",
    )(signal, grad_out, keys, queries, steps, decays, gains, pay, *inner)


def on_device(signal, step_size, log_decay, input_map, output_map, skip_gain, grad_out):
    args = (signal, grad_out, input_map, output_map, step_size, log_decay)
    pay = own_part(*args)
    mine = lax.all_to_all(pay, "ctx", 0, 0, tiled=True)
    inner = inner_part(*args)
    back = lax.all_to_all(scan_states(mine), "ctx", 0, 0, tiled=True)
    gs, gt, ga, gb, gc, gk = outer_part(*args, skip_gain.reshape(1, HEADS), back, inner)
    return gs, gt, ga, gb, gc, gk.reshape(HEADS)


def solution(mesh):
    placed = (
        P("ctx", "head"),
        P("head", "ctx"),
        P("head", "ctx"),
        P("ctx", "head"),
        P("ctx", "head"),
        P("head"),
        P("ctx", "head"),
    )
    return jax.shard_map(
        on_device,
        mesh=mesh,
        in_specs=placed,
        out_specs=(
            P("ctx", "head"),
            P("head", "ctx"),
            P("head", "ctx"),
            P("ctx", "head"),
            P("ctx", "head"),
            P("head"),
        ),
        check_vma=False,
    )
```

```python
import jax
import jax.numpy as jnp
from jax import lax
from jax.experimental import pallas as pl
from jax.experimental.pallas import tpu as pltpu
from jax.sharding import PartitionSpec as P

P_SIZE = 64
N = 128
HEADS = 16
Q = 128
T = 256
WIDE = HEADS * P_SIZE
ROWS = N + 8
LOG2E = 1.4426950408889634
NEG = -1e30
HIGH = lax.Precision.HIGHEST
f32 = jnp.float32
bf16 = jnp.bfloat16


def iota(shape, dim):
    return lax.broadcasted_iota(jnp.int32, shape, dim)


def split(z):
    hi = z.astype(bf16)
    lo = (z - hi.astype(f32)).astype(bf16)
    return hi, lo


def dot(a, b, ca, cb, precision=None):
    return lax.dot_general(
        a, b, (((ca,), (cb,)), ((), ())), precision=precision, preferred_element_type=f32
    )


def twice(a, axis):
    return jnp.concatenate([a, a], axis=axis)


def selector():
    return (iota((HEADS, WIDE), 1) // P_SIZE == iota((HEADS, WIDE), 0)).astype(f32).astype(bf16)


def paired(rows):
    return jnp.concatenate(split(rows), axis=0)


def expand(rows, sel2):
    return dot(paired(rows), sel2, 0, 0)


def per_head(z, sel):
    hi, lo = split(z)
    return dot(sel, hi, 1, 1) + dot(sel, lo, 1, 1)


def faded(state, fade):
    return (state.reshape(N // 8, 8, WIDE) * fade[None]).reshape(N, WIDE)


def folded(z):
    return jnp.sum(z.reshape(z.shape[0] // 8, 8, WIDE), axis=0)


def low_half(shape):
    return iota(shape, len(shape) - 1) < P_SIZE


def from_state(maps, state2):
    return dot(twice(maps, 1), state2, 1, 0)


def to_state(maps, hi, lo):
    return dot(twice(maps, 0), jnp.concatenate([hi, lo], axis=0), 0, 0)


def to_maps(hi, lo, state2):
    first = dot(hi, state2, 1, 1)
    return first[:, :N] + first[:, N:] + dot(lo, state2[:N], 1, 1)


def own_kernel(
    x_ref, dy_ref, b_ref, c_ref, dt_ref, a_ref,
    pay_ref, h_ref, cum_ref, tot_ref, tl_ref, ex_ref, p_ref, sk_ref, sel_ref,
):
    k = pl.program_id(0)
    count = a_ref.shape[1] // Q

    @pl.when(k == 0)
    def _():
        sk_ref[...] = jnp.zeros_like(sk_ref)
        sel_ref[...] = twice(selector(), 0)
        upper = (iota((Q, Q), 0) <= iota((Q, Q), 1)).astype(f32)
        stacked = jnp.concatenate([a_ref[:, Q * i : Q * (i + 1)] for i in range(count)], axis=0)
        sums = dot(stacked * LOG2E, upper, 1, 0, HIGH)
        run = jnp.zeros((HEADS, Q), f32)
        cums = []
        for i in range(count):
            cum = sums[HEADS * i : HEADS * (i + 1)]
            cum_ref[:, Q * i : Q * (i + 1)] = cum
            cums.append(cum + run)
            run = run + jnp.broadcast_to(cum[:, Q - 1 : Q], (HEADS, Q))
        tot_ref[...] = run
        for i in range(count):
            blk, off = (Q * i) // T, (Q * i) % T
            tails = jnp.exp2(run - cums[i]) * dt_ref[:, Q * i : Q * (i + 1)]
            tl_ref[blk, :, off : off + Q] = paired(tails)
            ex_ref[blk, :, off : off + Q] = paired(jnp.exp2(cums[i]))

    sel2 = sel_ref[...]
    x = x_ref[...].astype(f32)
    dy = dy_ref[...].astype(f32)
    xs = x * dot(tl_ref[k], sel2, 0, 0)
    ds = dy * dot(ex_ref[k], sel2, 0, 0)
    state = to_state(b_ref[...], *split(xs))
    pull = to_state(c_ref[...], *split(ds))
    sk_ref[...] = sk_ref[...] + folded(x * dy)

    @pl.when(k == 0)
    def _():
        h_ref[...] = state
        p_ref[...] = pull

    @pl.when(k > 0)
    def _():
        h_ref[...] = h_ref[...] + state
        p_ref[...] = p_ref[...] + pull

    @pl.when(k == pl.num_programs(0) - 1)
    def _():
        tot = tot_ref[...]
        skip = jnp.sum(
            dot(sel_ref[:HEADS].astype(f32), sk_ref[...], 1, 1, HIGH), axis=1, keepdims=True
        )
        skip = jnp.broadcast_to(skip, (HEADS, N))
        low = low_half((N, 128))
        row = iota((8, 128), 0)
        for j in range(HEADS // 2):
            hp = h_ref[:, 128 * j : 128 * (j + 1)]
            pp = p_ref[:, 128 * j : 128 * (j + 1)]
            pay_ref[2 * j, 0:N, :] = jnp.where(low, hp, pltpu.roll(pp, P_SIZE, 1))
            pay_ref[2 * j + 1, 0:N, :] = jnp.where(low, pltpu.roll(hp, P_SIZE, 1), pp)
        for h in range(HEADS):
            tail = jnp.where(row == 0, tot[h : h + 1, :], 0.0)
            pay_ref[h, N:ROWS, :] = jnp.where(row == 1, skip[h : h + 1, :], tail)


def whole(shape):
    return pl.BlockSpec(shape, lambda k: (0,) * len(shape))


def own_part(signal, grad_out, keys, queries, steps, decays):
    length = signal.shape[0]
    tok = lambda width: pl.BlockSpec((T, width), lambda k: (k, 0))
    outs = [
        ((HEADS, ROWS, 128), f32),
        ((N, WIDE), f32),
        ((HEADS, length), f32),
        ((HEADS, 128), f32),
        ((length // T, 2 * HEADS, T), bf16),
        ((length // T, 2 * HEADS, T), bf16),
    ]
    return pl.pallas_call(
        own_kernel,
        grid=(length // T,),
        in_specs=[tok(WIDE), tok(WIDE), tok(N), tok(N), whole(steps.shape), whole(steps.shape)],
        out_specs=[whole(shape) for shape, _ in outs],
        out_shape=[jax.ShapeDtypeStruct(*o) for o in outs],
        scratch_shapes=[
            pltpu.VMEM((N, WIDE), f32),
            pltpu.VMEM((8, WIDE), f32),
            pltpu.VMEM((2 * HEADS, WIDE), bf16),
        ],
        name="own_part",
    )(signal, grad_out, keys, queries, steps, decays)


def scan_kernel(pay_ref, out_ref):
    count = pay_ref.shape[0]
    low = low_half((N, 128))
    state = jnp.zeros((N, 128), f32)
    skip = jnp.zeros((8, 128), f32)
    for d in range(count):
        out_ref[d, 0:N, :] = state
        tail = pay_ref[d, N:ROWS, :]
        skip = skip + tail
        state = state * jnp.exp2(tail[0:1, :]) + pay_ref[d, 0:N, :]
    state = jnp.zeros((N, 128), f32)
    for d in reversed(range(count)):
        out_ref[d, 0:N, :] = jnp.where(low, out_ref[d, 0:N, :], state)
        out_ref[d, N:ROWS, :] = skip
        tail = pay_ref[d, N:ROWS, :]
        state = state * jnp.exp2(tail[0:1, :]) + pay_ref[d, 0:N, :]


def scan_states(pay):
    return pl.pallas_call(
        scan_kernel, out_shape=jax.ShapeDtypeStruct(pay.shape, f32), name="scan_states"
    )(pay)


def first_kernel(
    x_ref, dy_ref, b_ref, c_ref, dt_ref, cum_ref, u_ref, db_ref, dc_ref, r_ref, h_ref, sel_ref
):
    k = pl.program_id(0)

    @pl.when(k == 0)
    def _():
        h_ref[...] = jnp.zeros_like(h_ref)
        sel_ref[...] = twice(selector(), 0)

    cum = cum_ref[...]
    steps = dt_ref[...]
    keys = b_ref[...]
    queries = c_ref[...]
    sel2 = sel_ref[...]

    tot = jnp.broadcast_to(cum[:, Q - 1 : Q], (HEADS, Q))
    state = h_ref[...]
    state2 = paired(state)
    ds = dy_ref[...].astype(f32) * expand(jnp.exp2(cum), sel2)
    r_states = per_head(ds * from_state(queries, state2), sel2[:HEADS])
    dc_states = to_maps(*split(ds), state2)
    xs = x_ref[...].astype(f32) * expand(jnp.exp2(tot - cum) * steps, sel2)
    fade = expand(jnp.exp2(tot[:, :8]), sel2)
    h_ref[...] = faded(state, fade) + to_state(keys, *split(xs))

    col = jnp.transpose(cum - jnp.log2(steps))
    scores = dot(keys, queries, 1, 1)
    mask = iota((Q, Q), 0) <= iota((Q, Q), 1)
    low = low_half((Q, 128))
    mixed = jnp.zeros((Q, Q), f32)
    for j in range(HEADS // 2):
        lanes = slice(128 * j, 128 * (j + 1))
        dyp = dy_ref[:, lanes]
        zero = jnp.zeros_like(dyp)
        pair = jnp.concatenate([jnp.where(low, dyp, zero), jnp.where(low, zero, dyp)], axis=0)
        gram = dot(x_ref[:, lanes], pair, 1, 1)
        his, los = [], []
        for e in range(2):
            h = 2 * j + e
            g = gram[:, Q * e : Q * (e + 1)]
            decay = jnp.exp2(jnp.where(mask, cum[h : h + 1, :] - col[:, h : h + 1], NEG))
            weights = decay * scores
            mixed = mixed + decay * g
            r_ref[h : h + 1, :] = jnp.sum(weights * g, axis=0, keepdims=True)
            hi, lo = split(weights)
            his.append(hi)
            los.append(lo)
        both = jnp.concatenate(
            [jnp.concatenate(his, axis=1), jnp.concatenate(los, axis=1)], axis=0
        )
        out = dot(both, pair, 1, 0)
        u_ref[:, lanes] = out[:Q] + out[Q:]
    r_ref[...] = r_ref[...] + r_states
    parts = paired(mixed)
    db = dot(parts, queries, 1, 0)
    db_ref[...] = db[:Q] + db[Q:]
    dc_ref[...] = dc_states + dot(parts, twice(keys, 0), 0, 0)


def first_part(signal, grad_out, keys, queries, steps, cums):
    length = signal.shape[0]
    tok = lambda width: pl.BlockSpec((Q, width), lambda k: (k, 0))
    row = pl.BlockSpec((HEADS, Q), lambda k: (0, k))
    return pl.pallas_call(
        first_kernel,
        grid=(length // Q,),
        in_specs=[tok(WIDE), tok(WIDE), tok(N), tok(N), row, row],
        out_specs=[tok(WIDE), tok(N), tok(N), row],
        out_shape=[
            jax.ShapeDtypeStruct((length, WIDE), f32),
            jax.ShapeDtypeStruct((length, N), f32),
            jax.ShapeDtypeStruct((length, N), f32),
            jax.ShapeDtypeStruct((HEADS, length), f32),
        ],
        scratch_shapes=[pltpu.VMEM((N, WIDE), f32), pltpu.VMEM((2 * HEADS, WIDE), bf16)],
        name="first_part",
    )(signal, grad_out, keys, queries, steps, cums)


def second_kernel(
    x_ref, dy_ref, b_ref, c_ref, dt_ref, cum_ref, ui_ref, dbi_ref, u_ref, db_ref, g_ref, sel_ref
):
    k = pl.program_id(0)

    @pl.when(k == 0)
    def _():
        g_ref[...] = jnp.zeros_like(g_ref)
        sel_ref[...] = twice(selector(), 0)

    cum = cum_ref[...]
    sel2 = sel_ref[...]
    tot = jnp.broadcast_to(cum[:, Q - 1 : Q], (HEADS, Q))
    state = g_ref[...]
    state2 = paired(state)
    tails = expand(jnp.exp2(tot - cum) * dt_ref[...], sel2)
    u_ref[...] = ui_ref[...] + tails * from_state(b_ref[...], state2)
    db_ref[...] = dbi_ref[...] + to_maps(*split(x_ref[...].astype(f32) * tails), state2)
    ds = dy_ref[...].astype(f32) * expand(jnp.exp2(cum), sel2)
    fade = expand(jnp.exp2(tot[:, :8]), sel2)
    g_ref[...] = faded(state, fade) + to_state(c_ref[...], *split(ds))


def second_part(signal, grad_out, keys, queries, steps, cums, u, db):
    length = signal.shape[0]
    last = length // Q - 1
    tok = lambda width: pl.BlockSpec((Q, width), lambda k: (last - k, 0))
    row = pl.BlockSpec((HEADS, Q), lambda k: (0, last - k))
    return pl.pallas_call(
        second_kernel,
        grid=(length // Q,),
        in_specs=[tok(WIDE), tok(WIDE), tok(N), tok(N), row, row, tok(WIDE), tok(N)],
        out_specs=[tok(WIDE), tok(N)],
        out_shape=[
            jax.ShapeDtypeStruct((length, WIDE), f32),
            jax.ShapeDtypeStruct((length, N), f32),
        ],
        scratch_shapes=[pltpu.VMEM((N, WIDE), f32), pltpu.VMEM((2 * HEADS, WIDE), bf16)],
        name="second_part",
    )(signal, grad_out, keys, queries, steps, cums, u, db)


def last_kernel(
    x_ref, dy_ref, b_ref, c_ref, dt_ref, tl_ref, ex_ref, tot_ref, end_ref, gain_ref, pay_ref,
    ui_ref, dbi_ref, dci_ref, ri_ref,
    gs_ref, gt_ref, ga_ref, gb_ref, gc_ref, gk_ref, h_ref, g_ref, gains_ref, sel_ref, later_ref,
):
    k = pl.program_id(0)

    @pl.when(k == 0)
    def _():
        sel2 = twice(selector(), 0)
        sel_ref[...] = sel2
        low = low_half((N, 128))
        eye = iota((HEADS, 128), 0) == iota((HEADS, 128), 1)
        sums = jnp.zeros((HEADS, 128), f32)
        for h in range(HEADS):
            sums = jnp.where(iota((HEADS, 128), 0) == h, pay_ref[h, N + 1 : N + 2, :], sums)
        gk_ref[...] = jnp.sum(jnp.where(eye, sums, 0.0), axis=0, keepdims=True)[:, :HEADS]
        eye16 = iota((HEADS, HEADS), 0) == iota((HEADS, HEADS), 1)
        gains = jnp.sum(
            jnp.where(eye16, jnp.broadcast_to(gain_ref[...], (HEADS, HEADS)), 0.0),
            axis=1,
            keepdims=True,
        )
        gains_ref[...] = expand(jnp.broadcast_to(gains, (HEADS, 8)), sel2)
        fade = expand(jnp.exp2(tot_ref[:, :8]), sel2)
        ends = []
        for j in range(HEADS // 2):
            lanes = slice(128 * j, 128 * (j + 1))
            one = pay_ref[2 * j, 0:N, :]
            two = pay_ref[2 * j + 1, 0:N, :]
            h = jnp.where(low, one, pltpu.roll(two, P_SIZE, 1))
            g = jnp.where(low, pltpu.roll(one, P_SIZE, 1), two)
            h_ref[:, lanes] = paired(h)
            g_ref[:, lanes] = paired(g)
            end = (h.reshape(N // 8, 8, 128) * fade[None, :, lanes]).reshape(N, 128)
            end = (end + end_ref[:, lanes]) * g
            ends.append(jnp.sum(end.reshape(N // 8, 8, 128), axis=0))
        ends = jnp.concatenate(ends, axis=1)
        later = jnp.sum(dot(sel2[:HEADS].astype(f32), ends, 1, 1, HIGH), axis=1, keepdims=True)
        later_ref[...] = jnp.broadcast_to(later, (HEADS, 128))

    sel2 = sel_ref[...]
    sel = sel2[:HEADS]
    h2 = h_ref[...]
    g2 = g_ref[...]
    x = x_ref[...].astype(f32)
    dy = dy_ref[...].astype(f32)
    tails = dot(tl_ref[0], sel2, 0, 0)
    u = ui_ref[...] + tails * from_state(b_ref[...], g2)
    scaled = (dy.reshape(T // 8, 8, WIDE) * gains_ref[...][None]).reshape(T, WIDE)
    gs_ref[...] = (u + scaled).astype(bf16)
    cols = per_head(x * u, sel)
    gt_ref[...] = cols / dt_ref[...]
    gb_ref[...] = (dbi_ref[...] + to_maps(*split(x * tails), g2)).astype(bf16)
    ds = dy * dot(ex_ref[0], sel2, 0, 0)
    rows = ri_ref[...] + per_head(ds * from_state(c_ref[...], h2), sel)
    gc_ref[...] = (dci_ref[...] + to_maps(*split(ds), h2)).astype(bf16)
    lower = (iota((T, T), 0) >= iota((T, T), 1)).astype(f32)
    after = dot(rows - cols, lower, 1, 0, HIGH) + later_ref[:, 0:1]
    ga_ref[...] = after
    later_ref[...] = jnp.broadcast_to(after[:, 0:1], (HEADS, 128))


def last_part(
    signal, grad_out, keys, queries, steps, tails, expos, tot, end, gains, pay, u, db, dc, r
):
    length = signal.shape[0]
    last = length // T - 1
    tok = lambda width: pl.BlockSpec((T, width), lambda k: (last - k, 0))
    row = pl.BlockSpec((HEADS, T), lambda k: (0, last - k))
    scale = pl.BlockSpec((1, 2 * HEADS, T), lambda k: (last - k, 0, 0))
    return pl.pallas_call(
        last_kernel,
        grid=(length // T,),
        in_specs=[
            tok(WIDE), tok(WIDE), tok(N), tok(N), row, scale, scale, whole(tot.shape),
            whole(end.shape), whole(gains.shape), whole(pay.shape), tok(WIDE), tok(N), tok(N), row,
        ],
        out_specs=[tok(WIDE), row, row, tok(N), tok(N), whole((1, HEADS))],
        out_shape=[
            jax.ShapeDtypeStruct((length, WIDE), bf16),
            jax.ShapeDtypeStruct((HEADS, length), f32),
            jax.ShapeDtypeStruct((HEADS, length), f32),
            jax.ShapeDtypeStruct((length, N), bf16),
            jax.ShapeDtypeStruct((length, N), bf16),
            jax.ShapeDtypeStruct((1, HEADS), f32),
        ],
        scratch_shapes=[
            pltpu.VMEM((2 * N, WIDE), bf16),
            pltpu.VMEM((2 * N, WIDE), bf16),
            pltpu.VMEM((8, WIDE), f32),
            pltpu.VMEM((2 * HEADS, WIDE), bf16),
            pltpu.VMEM((HEADS, 128), f32),
        ],
        name="last_part",
    )(signal, grad_out, keys, queries, steps, tails, expos, tot, end, gains, pay, u, db, dc, r)


def on_device(signal, step_size, log_decay, input_map, output_map, skip_gain, grad_out):
    args = (signal, grad_out, input_map, output_map, step_size)
    pay, end, cums, tot, tails, expos = own_part(*args, log_decay)
    mine = lax.all_to_all(pay, "ctx", 0, 0, tiled=True)
    u, db, dc, r = first_part(*args, cums)
    mine, u = lax.optimization_barrier((mine, u))
    back = lax.all_to_all(scan_states(mine), "ctx", 0, 0, tiled=True)
    u, db = second_part(*args, cums, u, db)
    gs, gt, ga, gb, gc, gk = last_part(
        *args, tails, expos, tot, end, skip_gain.reshape(1, HEADS), back, u, db, dc, r
    )
    return gs, gt, ga, gb, gc, gk.reshape(HEADS)


def solution(mesh):
    placed = (
        P("ctx", "head"),
        P("head", "ctx"),
        P("head", "ctx"),
        P("ctx", "head"),
        P("ctx", "head"),
        P("head"),
        P("ctx", "head"),
    )
    return jax.shard_map(
        on_device,
        mesh=mesh,
        in_specs=placed,
        out_specs=(
            P("ctx", "head"),
            P("head", "ctx"),
            P("head", "ctx"),
            P("ctx", "head"),
            P("ctx", "head"),
            P("head"),
        ),
        check_vma=False,
    )
```

```python
import jax
import jax.numpy as jnp
from jax import lax
from jax.experimental import pallas as pl
from jax.experimental.pallas import tpu as pltpu
from jax.sharding import PartitionSpec as P

P_SIZE = 64
N = 128
HEADS = 16
Q = 128
T = 256
L = 256
HALF = N // 2
WIDE = HEADS * P_SIZE
ROWS = N + 8
LOG2E = 1.4426950408889634
NEG = -1e30
HIGH = lax.Precision.HIGHEST
f32 = jnp.float32
bf16 = jnp.bfloat16


def iota(shape, dim):
    return lax.broadcasted_iota(jnp.int32, shape, dim)


def split(z):
    hi = z.astype(bf16)
    lo = (z - hi.astype(f32)).astype(bf16)
    return hi, lo


def dot(a, b, ca, cb, precision=None):
    return lax.dot_general(
        a, b, (((ca,), (cb,)), ((), ())), precision=precision, preferred_element_type=f32
    )


def twice(a, axis):
    return jnp.concatenate([a, a], axis=axis)


def selector():
    return (iota((HEADS, WIDE), 1) // P_SIZE == iota((HEADS, WIDE), 0)).astype(f32).astype(bf16)


def paired(rows):
    return jnp.concatenate(split(rows), axis=0)


def expand(rows, sel2):
    return dot(paired(rows), sel2, 0, 0)


def per_head(z, sel):
    hi, lo = split(z)
    return dot(sel, hi, 1, 1) + dot(sel, lo, 1, 1)


def faded(state, fade):
    return (state.reshape(N // 8, 8, WIDE) * fade[None]).reshape(N, WIDE)


def folded(z):
    return jnp.sum(z.reshape(z.shape[0] // 8, 8, WIDE), axis=0)


def low_half(shape):
    return iota(shape, len(shape) - 1) < P_SIZE


def from_state(maps, state2):
    return dot(twice(maps, 1), state2, 1, 0)


def to_state(maps, hi, lo):
    return dot(twice(maps, 0), jnp.concatenate([hi, lo], axis=0), 0, 0)


def to_maps(hi, lo, state2):
    first = dot(hi, state2, 1, 1)
    return first[:, :N] + first[:, N:] + dot(lo, state2[:N], 1, 1)


def split3(z):
    hi = z.astype(bf16)
    rest = z - hi.astype(f32)
    mid = rest.astype(bf16)
    return jnp.concatenate([hi, mid, (rest - mid.astype(f32)).astype(bf16)], axis=0)


def times_ones(z, ones):
    out = dot(split3(z), ones.astype(f32).astype(bf16), 1, 0)
    size = z.shape[0]
    return out[:size] + out[size : 2 * size] + out[2 * size :]


def own_kernel(
    x_ref, dy_ref, b_ref, c_ref, dt_ref, a_ref,
    pay_ref, h_ref, cum_ref, fade_ref, tl_ref, ex_ref, p_ref, sk_ref, sel_ref,
):
    k = pl.program_id(0)
    count = a_ref.shape[1] // Q

    @pl.when(k == 0)
    def _():
        sk_ref[...] = jnp.zeros_like(sk_ref)
        h_ref[...] = jnp.zeros_like(h_ref)
        p_ref[...] = jnp.zeros_like(p_ref)
        sel = selector()
        sel_ref[...] = twice(sel, 0)
        stacked = jnp.concatenate([a_ref[:, Q * i : Q * (i + 1)] for i in range(count)], axis=0)
        sums = times_ones(stacked * LOG2E, iota((Q, Q), 0) <= iota((Q, Q), 1))
        run = jnp.zeros((HEADS, Q), f32)
        cums = []
        for i in range(count):
            cum = sums[HEADS * i : HEADS * (i + 1)]
            cum_ref[:, Q * i : Q * (i + 1)] = cum
            cums.append(cum + run)
            run = run + jnp.broadcast_to(cum[:, Q - 1 : Q], (HEADS, Q))
        fade_ref[...] = dot(split3(jnp.exp2(run[:, :8])), jnp.concatenate([sel] * 3, axis=0), 0, 0)
        for i in range(count):
            blk, off = (Q * i) // T, (Q * i) % T
            tails = jnp.exp2(run - cums[i]) * dt_ref[:, Q * i : Q * (i + 1)]
            tl_ref[blk, :, off : off + Q] = paired(tails)
            ex_ref[blk, :, off : off + Q] = paired(jnp.exp2(cums[i]))

    tails = tl_ref[k]
    expos = ex_ref[k]
    keys = b_ref[...]
    queries = c_ref[...]
    for i in range(WIDE // L):
        lanes = slice(L * i, L * (i + 1))
        sel2 = sel_ref[:, lanes]
        x = x_ref[:, lanes].astype(f32)
        h_ref[:, lanes] += to_state(keys, *split(x * dot(tails, sel2, 0, 0)))
        dy = dy_ref[:, lanes].astype(f32)
        p_ref[:, lanes] += to_state(queries, *split(dy * dot(expos, sel2, 0, 0)))
        sk_ref[:, lanes] += jnp.sum((x * dy).reshape(T // 8, 8, L), axis=0)

    @pl.when(k == pl.num_programs(0) - 1)
    def _():
        first = iota((8, 128), 0) == 0
        second = iota((8, 128), 0) == 1
        for j in range(HEADS // 2):
            lanes = slice(128 * j, 128 * (j + 1))
            skip = jnp.sum(sk_ref[:, lanes], axis=0, keepdims=True)
            tail = jnp.where(first, fade_ref[:, lanes], jnp.where(second, skip, 0.0))
            for e in range(2):
                rows = slice(HALF * e, HALF * (e + 1))
                pay_ref[2 * j + e, 0:HALF, :] = h_ref[rows, lanes]
                pay_ref[2 * j + e, HALF:N, :] = p_ref[rows, lanes]
                pay_ref[2 * j + e, N:ROWS, :] = tail


def whole(shape):
    return pl.BlockSpec(shape, lambda k: (0,) * len(shape))


def own_part(signal, grad_out, keys, queries, steps, decays):
    length = signal.shape[0]
    tok = lambda width: pl.BlockSpec((T, width), lambda k: (k, 0))
    outs = [
        ((HEADS, ROWS, 128), f32),
        ((N, WIDE), f32),
        ((HEADS, length), f32),
        ((8, WIDE), f32),
        ((length // T, 2 * HEADS, T), bf16),
        ((length // T, 2 * HEADS, T), bf16),
    ]
    return pl.pallas_call(
        own_kernel,
        grid=(length // T,),
        in_specs=[tok(WIDE), tok(WIDE), tok(N), tok(N), whole(steps.shape), whole(steps.shape)],
        out_specs=[whole(shape) for shape, _ in outs],
        out_shape=[jax.ShapeDtypeStruct(*o) for o in outs],
        scratch_shapes=[
            pltpu.VMEM((N, WIDE), f32),
            pltpu.VMEM((8, WIDE), f32),
            pltpu.VMEM((2 * HEADS, WIDE), bf16),
        ],
        name="own_part",
    )(signal, grad_out, keys, queries, steps, decays)


def scan_kernel(pay_ref, out_ref):
    count = pay_ref.shape[0]
    state = jnp.zeros((HALF, 128), f32)
    skip = jnp.zeros((8, 128), f32)
    for d in range(count):
        out_ref[d, 0:HALF, :] = state
        tail = pay_ref[d, N:ROWS, :]
        skip = skip + tail
        state = state * tail[0:1, :] + pay_ref[d, 0:HALF, :]
    state = jnp.zeros((HALF, 128), f32)
    for d in reversed(range(count)):
        out_ref[d, HALF:N, :] = state
        out_ref[d, N:ROWS, :] = skip
        state = state * pay_ref[d, N : N + 1, :] + pay_ref[d, HALF:N, :]


def scan_states(pay):
    return pl.pallas_call(
        scan_kernel,
        in_specs=[pl.BlockSpec(memory_space=pltpu.VMEM)],
        out_specs=pl.BlockSpec(memory_space=pltpu.VMEM),
        out_shape=jax.ShapeDtypeStruct(pay.shape, f32),
        name="scan_states",
    )(pay)


def first_kernel(
    x_ref, dy_ref, b_ref, c_ref, dt_ref, cum_ref, u_ref, db_ref, dc_ref, r_ref, h_ref, sel_ref
):
    k = pl.program_id(0)

    @pl.when(k == 0)
    def _():
        h_ref[...] = jnp.zeros_like(h_ref)
        sel_ref[...] = twice(selector(), 0)

    cum = cum_ref[...]
    steps = dt_ref[...]
    keys = b_ref[...]
    queries = c_ref[...]
    sel2 = sel_ref[...]

    tot = jnp.broadcast_to(cum[:, Q - 1 : Q], (HEADS, Q))
    state = h_ref[...]
    state2 = paired(state)
    ds = dy_ref[...].astype(f32) * expand(jnp.exp2(cum), sel2)
    r_states = per_head(ds * from_state(queries, state2), sel2[:HEADS])
    dc_states = to_maps(*split(ds), state2)
    xs = x_ref[...].astype(f32) * expand(jnp.exp2(tot - cum) * steps, sel2)
    fade = expand(jnp.exp2(tot[:, :8]), sel2)
    h_ref[...] = faded(state, fade) + to_state(keys, *split(xs))

    col = jnp.transpose(cum - jnp.log2(steps))
    scores = dot(keys, queries, 1, 1)
    mask = iota((Q, Q), 0) <= iota((Q, Q), 1)
    low = low_half((Q, 128))
    mixed = jnp.zeros((Q, Q), f32)
    for j in range(HEADS // 2):
        lanes = slice(128 * j, 128 * (j + 1))
        dyp = dy_ref[:, lanes]
        zero = jnp.zeros_like(dyp)
        pair = jnp.concatenate([jnp.where(low, dyp, zero), jnp.where(low, zero, dyp)], axis=0)
        gram = dot(x_ref[:, lanes], pair, 1, 1)
        his, los = [], []
        for e in range(2):
            h = 2 * j + e
            g = gram[:, Q * e : Q * (e + 1)]
            decay = jnp.exp2(jnp.where(mask, cum[h : h + 1, :] - col[:, h : h + 1], NEG))
            weights = decay * scores
            mixed = mixed + decay * g
            r_ref[h : h + 1, :] = jnp.sum(weights * g, axis=0, keepdims=True)
            hi, lo = split(weights)
            his.append(hi)
            los.append(lo)
        both = jnp.concatenate(
            [jnp.concatenate(his, axis=1), jnp.concatenate(los, axis=1)], axis=0
        )
        out = dot(both, pair, 1, 0)
        u_ref[:, lanes] = out[:Q] + out[Q:]
    r_ref[...] = r_ref[...] + r_states
    parts = paired(mixed)
    db = dot(parts, queries, 1, 0)
    db_ref[...] = db[:Q] + db[Q:]
    dc_ref[...] = dc_states + dot(parts, twice(keys, 0), 0, 0)


def first_part(signal, grad_out, keys, queries, steps, cums):
    length = signal.shape[0]
    tok = lambda width: pl.BlockSpec((Q, width), lambda k: (k, 0))
    row = pl.BlockSpec((HEADS, Q), lambda k: (0, k))
    return pl.pallas_call(
        first_kernel,
        grid=(length // Q,),
        in_specs=[tok(WIDE), tok(WIDE), tok(N), tok(N), row, row],
        out_specs=[tok(WIDE), tok(N), tok(N), row],
        out_shape=[
            jax.ShapeDtypeStruct((length, WIDE), f32),
            jax.ShapeDtypeStruct((length, N), f32),
            jax.ShapeDtypeStruct((length, N), f32),
            jax.ShapeDtypeStruct((HEADS, length), f32),
        ],
        scratch_shapes=[pltpu.VMEM((N, WIDE), f32), pltpu.VMEM((2 * HEADS, WIDE), bf16)],
        name="first_part",
    )(signal, grad_out, keys, queries, steps, cums)


def second_kernel(
    x_ref, dy_ref, b_ref, c_ref, dt_ref, cum_ref, ui_ref, dbi_ref, u_ref, db_ref, g_ref, sel_ref
):
    k = pl.program_id(0)

    @pl.when(k == 0)
    def _():
        g_ref[...] = jnp.zeros_like(g_ref)
        sel_ref[...] = twice(selector(), 0)

    cum = cum_ref[...]
    sel2 = sel_ref[...]
    tot = jnp.broadcast_to(cum[:, Q - 1 : Q], (HEADS, Q))
    state = g_ref[...]
    state2 = paired(state)
    tails = expand(jnp.exp2(tot - cum) * dt_ref[...], sel2)
    u_ref[...] = ui_ref[...] + tails * from_state(b_ref[...], state2)
    db_ref[...] = dbi_ref[...] + to_maps(*split(x_ref[...].astype(f32) * tails), state2)
    ds = dy_ref[...].astype(f32) * expand(jnp.exp2(cum), sel2)
    fade = expand(jnp.exp2(tot[:, :8]), sel2)
    g_ref[...] = faded(state, fade) + to_state(c_ref[...], *split(ds))


def second_part(signal, grad_out, keys, queries, steps, cums, u, db):
    length = signal.shape[0]
    last = length // Q - 1
    tok = lambda width: pl.BlockSpec((Q, width), lambda k: (last - k, 0))
    row = pl.BlockSpec((HEADS, Q), lambda k: (0, last - k))
    return pl.pallas_call(
        second_kernel,
        grid=(length // Q,),
        in_specs=[tok(WIDE), tok(WIDE), tok(N), tok(N), row, row, tok(WIDE), tok(N)],
        out_specs=[tok(WIDE), tok(N)],
        out_shape=[
            jax.ShapeDtypeStruct((length, WIDE), f32),
            jax.ShapeDtypeStruct((length, N), f32),
        ],
        scratch_shapes=[pltpu.VMEM((N, WIDE), f32), pltpu.VMEM((2 * HEADS, WIDE), bf16)],
        name="second_part",
    )(signal, grad_out, keys, queries, steps, cums, u, db)


def last_kernel(
    x_ref, dy_ref, b_ref, c_ref, dt_ref, tl_ref, ex_ref, fade_ref, end_ref, gain_ref, pay_ref,
    ui_ref, dbi_ref, dci_ref, ri_ref,
    gs_ref, gt_ref, ga_ref, gb_ref, gc_ref, gk_ref,
    h_ref, g_ref, gains_ref, sel_ref, later_ref, xh_ref, xl_ref, dh_ref, dl_ref,
):
    k = pl.program_id(0)

    @pl.when(k == 0)
    def _():
        sel = selector()
        sel2 = twice(sel, 0)
        sel_ref[...] = sel2
        eye16 = iota((HEADS, HEADS), 0) == iota((HEADS, HEADS), 1)
        gains = jnp.sum(
            jnp.where(eye16, jnp.broadcast_to(gain_ref[...], (HEADS, HEADS)), 0.0),
            axis=1,
            keepdims=True,
        )
        gains_ref[...] = expand(jnp.broadcast_to(gains, (HEADS, 8)), sel2)
        ends = []
        sums = []
        for j in range(HEADS // 2):
            lanes = slice(128 * j, 128 * (j + 1))
            sums.append(pay_ref[2 * j, N + 1 : N + 2, :])
            total = jnp.zeros((8, 128), f32)
            for e in range(2):
                rows = slice(HALF * e, HALF * (e + 1))
                low_rows = slice(N + HALF * e, N + HALF * (e + 1))
                h = pay_ref[2 * j + e, 0:HALF, :]
                g = pay_ref[2 * j + e, HALF:N, :]
                h_ref[rows, lanes], h_ref[low_rows, lanes] = split(h)
                g_ref[rows, lanes], g_ref[low_rows, lanes] = split(g)
                end = (h.reshape(HALF // 8, 8, 128) * fade_ref[:, lanes][None]).reshape(HALF, 128)
                end = (end + end_ref[rows, lanes]) * g
                total = total + jnp.sum(end.reshape(HALF // 8, 8, 128), axis=0)
            ends.append(total)
        ends = jnp.concatenate(ends, axis=1)
        later = jnp.sum(dot(sel, split3(ends), 1, 1), axis=1, keepdims=True)
        later_ref[...] = jnp.broadcast_to(later, (HEADS, 128))
        sums = jnp.concatenate(sums, axis=0)
        low = low_half(sums.shape)
        even = jnp.sum(jnp.where(low, sums, 0.0), axis=1, keepdims=True)
        odd = jnp.sum(jnp.where(low, 0.0, sums), axis=1, keepdims=True)
        row, lane = iota((HEADS // 2, HEADS), 0), iota((HEADS // 2, HEADS), 1)
        skips = jnp.where(lane == 2 * row, even, jnp.where(lane == 2 * row + 1, odd, 0.0))
        gk_ref[...] = jnp.sum(skips, axis=0, keepdims=True)

    keys2 = twice(b_ref[...], 1)
    queries2 = twice(c_ref[...], 1)
    tails_row = tl_ref[0]
    expos_row = ex_ref[0]
    cols = jnp.zeros((HEADS, T), f32)
    rows = ri_ref[...]
    for i in range(WIDE // L):
        lanes = slice(L * i, L * (i + 1))
        sel2 = sel_ref[:, lanes]
        sel = sel_ref[:HEADS, lanes]
        x = x_ref[:, lanes].astype(f32)
        tails = dot(tails_row, sel2, 0, 0)
        u = ui_ref[:, lanes] + tails * dot(keys2, g_ref[:, lanes], 1, 0)
        xh_ref[:, lanes], xl_ref[:, lanes] = split(x * tails)
        cols = cols + per_head(x * u, sel)
        dy = dy_ref[:, lanes].astype(f32)
        scaled = (dy.reshape(T // 8, 8, L) * gains_ref[:, lanes][None]).reshape(T, L)
        gs_ref[:, lanes] = (u + scaled).astype(bf16)
        ds = dy * dot(expos_row, sel2, 0, 0)
        dh_ref[:, lanes], dl_ref[:, lanes] = split(ds)
        rows = rows + per_head(ds * dot(queries2, h_ref[:, lanes], 1, 0), sel)
    gt_ref[...] = cols / dt_ref[...]
    gb_ref[...] = (dbi_ref[...] + to_maps(xh_ref[...], xl_ref[...], g_ref[...])).astype(bf16)
    gc_ref[...] = (dci_ref[...] + to_maps(dh_ref[...], dl_ref[...], h_ref[...])).astype(bf16)
    after = times_ones(rows - cols, iota((T, T), 0) >= iota((T, T), 1)) + later_ref[:, 0:1]
    ga_ref[...] = after
    later_ref[...] = jnp.broadcast_to(after[:, 0:1], (HEADS, 128))


def last_part(
    signal, grad_out, keys, queries, steps, tails, expos, fade, end, gains, pay, u, db, dc, r
):
    length = signal.shape[0]
    last = length // T - 1
    tok = lambda width: pl.BlockSpec((T, width), lambda k: (last - k, 0))
    row = pl.BlockSpec((HEADS, T), lambda k: (0, last - k))
    scale = pl.BlockSpec((1, 2 * HEADS, T), lambda k: (last - k, 0, 0))
    return pl.pallas_call(
        last_kernel,
        grid=(length // T,),
        in_specs=[
            tok(WIDE), tok(WIDE), tok(N), tok(N), row, scale, scale, whole(fade.shape),
            whole(end.shape), whole(gains.shape), pl.BlockSpec(memory_space=pltpu.VMEM),
            tok(WIDE), tok(N), tok(N), row,
        ],
        out_specs=[tok(WIDE), row, row, tok(N), tok(N), whole((1, HEADS))],
        out_shape=[
            jax.ShapeDtypeStruct((length, WIDE), bf16),
            jax.ShapeDtypeStruct((HEADS, length), f32),
            jax.ShapeDtypeStruct((HEADS, length), f32),
            jax.ShapeDtypeStruct((length, N), bf16),
            jax.ShapeDtypeStruct((length, N), bf16),
            jax.ShapeDtypeStruct((1, HEADS), f32),
        ],
        scratch_shapes=[
            pltpu.VMEM((2 * N, WIDE), bf16),
            pltpu.VMEM((2 * N, WIDE), bf16),
            pltpu.VMEM((8, WIDE), f32),
            pltpu.VMEM((2 * HEADS, WIDE), bf16),
            pltpu.VMEM((HEADS, 128), f32),
            pltpu.VMEM((T, WIDE), bf16),
            pltpu.VMEM((T, WIDE), bf16),
            pltpu.VMEM((T, WIDE), bf16),
            pltpu.VMEM((T, WIDE), bf16),
        ],
        name="last_part",
    )(signal, grad_out, keys, queries, steps, tails, expos, fade, end, gains, pay, u, db, dc, r)


def on_device(signal, step_size, log_decay, input_map, output_map, skip_gain, grad_out):
    args = (signal, grad_out, input_map, output_map, step_size)
    pay, end, cums, fade, tails, expos = own_part(*args, log_decay)
    mine = lax.all_to_all(pay, "ctx", 0, 0, tiled=True)
    u, db, dc, r = first_part(*args, cums)
    mine, u = lax.optimization_barrier((mine, u))
    back = lax.all_to_all(scan_states(mine), "ctx", 0, 0, tiled=True)
    u, db = second_part(*args, cums, u, db)
    gs, gt, ga, gb, gc, gk = last_part(
        *args, tails, expos, fade, end, skip_gain.reshape(1, HEADS), back, u, db, dc, r
    )
    return gs, gt, ga, gb, gc, gk.reshape(HEADS)


def solution(mesh):
    placed = (
        P("ctx", "head"),
        P("head", "ctx"),
        P("head", "ctx"),
        P("ctx", "head"),
        P("ctx", "head"),
        P("head"),
        P("ctx", "head"),
    )
    return jax.shard_map(
        on_device,
        mesh=mesh,
        in_specs=placed,
        out_specs=(
            P("ctx", "head"),
            P("head", "ctx"),
            P("head", "ctx"),
            P("ctx", "head"),
            P("ctx", "head"),
            P("head"),
        ),
        check_vma=False,
    )
```

```python
import jax
import jax.numpy as jnp
from jax import lax
from jax.experimental import pallas as pl
from jax.experimental.pallas import tpu as pltpu
from jax.sharding import PartitionSpec as P

P_SIZE = 64
N = 128
HEADS = 16
Q = 128
T = 256
L = 256
HALF = N // 2
PAIRS = HEADS // 2
EARLY = 6
WIDE = HEADS * P_SIZE
ROWS = N + 8
LOG2E = 1.4426950408889634
NEG = -1e30
HIGH = lax.Precision.HIGHEST
f32 = jnp.float32
bf16 = jnp.bfloat16


def iota(shape, dim):
    return lax.broadcasted_iota(jnp.int32, shape, dim)


def split(z):
    hi = z.astype(bf16)
    lo = (z - hi.astype(f32)).astype(bf16)
    return hi, lo


def dot(a, b, ca, cb, precision=None):
    return lax.dot_general(
        a, b, (((ca,), (cb,)), ((), ())), precision=precision, preferred_element_type=f32
    )


def twice(a, axis):
    return jnp.concatenate([a, a], axis=axis)


def selector():
    return (iota((HEADS, WIDE), 1) // P_SIZE == iota((HEADS, WIDE), 0)).astype(f32).astype(bf16)


def paired(rows):
    return jnp.concatenate(split(rows), axis=0)


def expand(rows, sel2):
    return dot(paired(rows), sel2, 0, 0)


def per_head(z, sel):
    hi, lo = split(z)
    return dot(sel, hi, 1, 1) + dot(sel, lo, 1, 1)


def faded(state, fade):
    return (state.reshape(N // 8, 8, WIDE) * fade[None]).reshape(N, WIDE)


def folded(z):
    return jnp.sum(z.reshape(z.shape[0] // 8, 8, WIDE), axis=0)


def low_half(shape):
    return iota(shape, len(shape) - 1) < P_SIZE


def from_state(maps, state2):
    return dot(twice(maps, 1), state2, 1, 0)


def to_state(maps, hi, lo):
    return dot(twice(maps, 0), jnp.concatenate([hi, lo], axis=0), 0, 0)


def to_maps(hi, lo, state2):
    first = dot(hi, state2, 1, 1)
    return first[:, :N] + first[:, N:] + dot(lo, state2[:N], 1, 1)


def split3(z):
    hi = z.astype(bf16)
    rest = z - hi.astype(f32)
    mid = rest.astype(bf16)
    return jnp.concatenate([hi, mid, (rest - mid.astype(f32)).astype(bf16)], axis=0)


def times_ones(z, ones):
    out = dot(split3(z), ones.astype(f32).astype(bf16), 1, 0)
    size = z.shape[0]
    return out[:size] + out[size : 2 * size] + out[2 * size :]


def own_kernel(
    x_ref, dy_ref, b_ref, c_ref, dt_ref, a_ref,
    pay_ref, h_ref, cum_ref, fade_ref, tl_ref, ex_ref, p_ref, sk_ref, sel_ref,
):
    k = pl.program_id(0)
    count = a_ref.shape[1] // Q

    @pl.when(k == 0)
    def _():
        sk_ref[...] = jnp.zeros_like(sk_ref)
        h_ref[...] = jnp.zeros_like(h_ref)
        p_ref[...] = jnp.zeros_like(p_ref)
        sel = selector()
        sel_ref[...] = twice(sel, 0)
        stacked = jnp.concatenate([a_ref[:, Q * i : Q * (i + 1)] for i in range(count)], axis=0)
        sums = times_ones(stacked * LOG2E, iota((Q, Q), 0) <= iota((Q, Q), 1))
        run = jnp.zeros((HEADS, Q), f32)
        cums = []
        for i in range(count):
            cum = sums[HEADS * i : HEADS * (i + 1)]
            cum_ref[:, Q * i : Q * (i + 1)] = cum
            cums.append(cum + run)
            run = run + jnp.broadcast_to(cum[:, Q - 1 : Q], (HEADS, Q))
        fade_ref[...] = dot(split3(jnp.exp2(run[:, :8])), jnp.concatenate([sel] * 3, axis=0), 0, 0)
        for i in range(count):
            blk, off = (Q * i) // T, (Q * i) % T
            tails = jnp.exp2(run - cums[i]) * dt_ref[:, Q * i : Q * (i + 1)]
            tl_ref[blk, :, off : off + Q] = paired(tails)
            ex_ref[blk, :, off : off + Q] = paired(jnp.exp2(cums[i]))

    tails = tl_ref[k]
    expos = ex_ref[k]
    keys = b_ref[...]
    queries = c_ref[...]
    for i in range(WIDE // L):
        lanes = slice(L * i, L * (i + 1))
        sel2 = sel_ref[:, lanes]
        x = x_ref[:, lanes].astype(f32)
        h_ref[:, lanes] += to_state(keys, *split(x * dot(tails, sel2, 0, 0)))
        dy = dy_ref[:, lanes].astype(f32)
        p_ref[:, lanes] += to_state(queries, *split(dy * dot(expos, sel2, 0, 0)))
        sk_ref[:, lanes] += jnp.sum((x * dy).reshape(T // 8, 8, L), axis=0)

    @pl.when(k == pl.num_programs(0) - 1)
    def _():
        first = iota((8, 128), 0) == 0
        second = iota((8, 128), 0) == 1
        for j in range(HEADS // 2):
            lanes = slice(128 * j, 128 * (j + 1))
            skip = jnp.sum(sk_ref[:, lanes], axis=0, keepdims=True)
            tail = jnp.where(first, fade_ref[:, lanes], jnp.where(second, skip, 0.0))
            for e in range(2):
                rows = slice(HALF * e, HALF * (e + 1))
                pay_ref[2 * j + e, 0:HALF, :] = h_ref[rows, lanes]
                pay_ref[2 * j + e, HALF:N, :] = p_ref[rows, lanes]
                pay_ref[2 * j + e, N:ROWS, :] = tail


def whole(shape):
    return pl.BlockSpec(shape, lambda k: (0,) * len(shape))


def own_part(signal, grad_out, keys, queries, steps, decays):
    length = signal.shape[0]
    tok = lambda width: pl.BlockSpec((T, width), lambda k: (k, 0))
    outs = [
        ((HEADS, ROWS, 128), f32),
        ((N, WIDE), f32),
        ((HEADS, length), f32),
        ((8, WIDE), f32),
        ((length // T, 2 * HEADS, T), bf16),
        ((length // T, 2 * HEADS, T), bf16),
    ]
    return pl.pallas_call(
        own_kernel,
        grid=(length // T,),
        in_specs=[tok(WIDE), tok(WIDE), tok(N), tok(N), whole(steps.shape), whole(steps.shape)],
        out_specs=[whole(shape) for shape, _ in outs],
        out_shape=[jax.ShapeDtypeStruct(*o) for o in outs],
        scratch_shapes=[
            pltpu.VMEM((N, WIDE), f32),
            pltpu.VMEM((8, WIDE), f32),
            pltpu.VMEM((2 * HEADS, WIDE), bf16),
        ],
        name="own_part",
    )(signal, grad_out, keys, queries, steps, decays)


def scan_kernel(pay_ref, out_ref):
    count = pay_ref.shape[0]
    state = jnp.zeros((HALF, 128), f32)
    skip = jnp.zeros((8, 128), f32)
    for d in range(count):
        out_ref[d, 0:HALF, :] = state
        tail = pay_ref[d, N:ROWS, :]
        skip = skip + tail
        state = state * tail[0:1, :] + pay_ref[d, 0:HALF, :]
    state = jnp.zeros((HALF, 128), f32)
    for d in reversed(range(count)):
        out_ref[d, HALF:N, :] = state
        out_ref[d, N:ROWS, :] = skip
        state = state * pay_ref[d, N : N + 1, :] + pay_ref[d, HALF:N, :]


def scan_states(pay):
    return pl.pallas_call(
        scan_kernel,
        in_specs=[pl.BlockSpec(memory_space=pltpu.VMEM)],
        out_specs=pl.BlockSpec(memory_space=pltpu.VMEM),
        out_shape=jax.ShapeDtypeStruct(pay.shape, f32),
        name="scan_states",
    )(pay)


def inner_pairs(x_ref, dy_ref, keys, queries, cum, steps, pairs, r_ref):
    col = jnp.transpose(cum - jnp.log2(steps))
    scores = dot(keys, queries, 1, 1)
    mask = iota((Q, Q), 0) <= iota((Q, Q), 1)
    low = low_half((Q, 128))
    mixed = jnp.zeros((Q, Q), f32)
    us = []
    for j in pairs:
        lanes = slice(128 * j, 128 * (j + 1))
        dyp = dy_ref[:, lanes]
        zero = jnp.zeros_like(dyp)
        pair = jnp.concatenate([jnp.where(low, dyp, zero), jnp.where(low, zero, dyp)], axis=0)
        gram = dot(x_ref[:, lanes], pair, 1, 1)
        his, los = [], []
        for e in range(2):
            h = 2 * j + e
            g = gram[:, Q * e : Q * (e + 1)]
            decay = jnp.exp2(jnp.where(mask, cum[h : h + 1, :] - col[:, h : h + 1], NEG))
            weights = decay * scores
            mixed = mixed + decay * g
            r_ref[h : h + 1, :] += jnp.sum(weights * g, axis=0, keepdims=True)
            hi, lo = split(weights)
            his.append(hi)
            los.append(lo)
        both = jnp.concatenate(
            [jnp.concatenate(his, axis=1), jnp.concatenate(los, axis=1)], axis=0
        )
        out = dot(both, pair, 1, 0)
        us.append(out[:Q] + out[Q:])
    parts = paired(mixed)
    db = dot(parts, queries, 1, 0)
    return us, db[:Q] + db[Q:], dot(parts, twice(keys, 0), 0, 0)


def first_kernel(
    x_ref, dy_ref, b_ref, c_ref, dt_ref, cum_ref, u_ref, db_ref, dc_ref, r_ref, h_ref, sel_ref
):
    k = pl.program_id(0)

    @pl.when(k == 0)
    def _():
        h_ref[...] = jnp.zeros_like(h_ref)
        sel_ref[...] = twice(selector(), 0)

    cum = cum_ref[...]
    steps = dt_ref[...]
    keys = b_ref[...]
    queries = c_ref[...]
    sel2 = sel_ref[...]

    tot = jnp.broadcast_to(cum[:, Q - 1 : Q], (HEADS, Q))
    state = h_ref[...]
    state2 = paired(state)
    ds = dy_ref[...].astype(f32) * expand(jnp.exp2(cum), sel2)
    r_states = per_head(ds * from_state(queries, state2), sel2[:HEADS])
    dc_states = to_maps(*split(ds), state2)
    xs = x_ref[...].astype(f32) * expand(jnp.exp2(tot - cum) * steps, sel2)
    fade = expand(jnp.exp2(tot[:, :8]), sel2)
    h_ref[...] = faded(state, fade) + to_state(keys, *split(xs))

    r_ref[...] = r_states
    us, db, dc = inner_pairs(x_ref, dy_ref, keys, queries, cum, steps, range(EARLY), r_ref)
    for j, u in enumerate(us):
        u_ref[:, 128 * j : 128 * (j + 1)] = u
    db_ref[...] = db
    dc_ref[...] = dc_states + dc


def first_part(signal, grad_out, keys, queries, steps, cums):
    length = signal.shape[0]
    tok = lambda width: pl.BlockSpec((Q, width), lambda k: (k, 0))
    row = pl.BlockSpec((HEADS, Q), lambda k: (0, k))
    return pl.pallas_call(
        first_kernel,
        grid=(length // Q,),
        in_specs=[tok(WIDE), tok(WIDE), tok(N), tok(N), row, row],
        out_specs=[tok(WIDE), tok(N), tok(N), row],
        out_shape=[
            jax.ShapeDtypeStruct((length, WIDE), f32),
            jax.ShapeDtypeStruct((length, N), f32),
            jax.ShapeDtypeStruct((length, N), f32),
            jax.ShapeDtypeStruct((HEADS, length), f32),
        ],
        scratch_shapes=[pltpu.VMEM((N, WIDE), f32), pltpu.VMEM((2 * HEADS, WIDE), bf16)],
        name="first_part",
    )(signal, grad_out, keys, queries, steps, cums)


def second_kernel(
    x_ref, dy_ref, b_ref, c_ref, dt_ref, cum_ref, ui_ref, dbi_ref, dci_ref, ri_ref,
    u_ref, db_ref, dc_ref, r_ref, g_ref, sel_ref,
):
    k = pl.program_id(0)

    @pl.when(k == 0)
    def _():
        g_ref[...] = jnp.zeros_like(g_ref)
        sel_ref[...] = twice(selector(), 0)

    cum = cum_ref[...]
    steps = dt_ref[...]
    keys = b_ref[...]
    queries = c_ref[...]
    sel2 = sel_ref[...]
    tot = jnp.broadcast_to(cum[:, Q - 1 : Q], (HEADS, Q))
    state = g_ref[...]
    state2 = paired(state)
    tails = expand(jnp.exp2(tot - cum) * steps, sel2)
    passed = tails * from_state(keys, state2)
    db_states = to_maps(*split(x_ref[...].astype(f32) * tails), state2)
    ds = dy_ref[...].astype(f32) * expand(jnp.exp2(cum), sel2)
    fade = expand(jnp.exp2(tot[:, :8]), sel2)
    g_ref[...] = faded(state, fade) + to_state(queries, *split(ds))

    r_ref[...] = ri_ref[...]
    pairs = range(EARLY, PAIRS)
    us, db, dc = inner_pairs(x_ref, dy_ref, keys, queries, cum, steps, pairs, r_ref)
    done = 128 * EARLY
    u_ref[:, :done] = ui_ref[:, :done] + passed[:, :done]
    for j, u in zip(pairs, us):
        lanes = slice(128 * j, 128 * (j + 1))
        u_ref[:, lanes] = passed[:, lanes] + u
    db_ref[...] = dbi_ref[...] + db_states + db
    dc_ref[...] = dci_ref[...] + dc


def second_part(signal, grad_out, keys, queries, steps, cums, u, db, dc, r):
    length = signal.shape[0]
    last = length // Q - 1
    tok = lambda width: pl.BlockSpec((Q, width), lambda k: (last - k, 0))
    row = pl.BlockSpec((HEADS, Q), lambda k: (0, last - k))
    return pl.pallas_call(
        second_kernel,
        grid=(length // Q,),
        in_specs=[
            tok(WIDE), tok(WIDE), tok(N), tok(N), row, row, tok(WIDE), tok(N), tok(N), row,
        ],
        out_specs=[tok(WIDE), tok(N), tok(N), row],
        out_shape=[
            jax.ShapeDtypeStruct((length, WIDE), f32),
            jax.ShapeDtypeStruct((length, N), f32),
            jax.ShapeDtypeStruct((length, N), f32),
            jax.ShapeDtypeStruct((HEADS, length), f32),
        ],
        scratch_shapes=[pltpu.VMEM((N, WIDE), f32), pltpu.VMEM((2 * HEADS, WIDE), bf16)],
        name="second_part",
    )(signal, grad_out, keys, queries, steps, cums, u, db, dc, r)


def last_kernel(
    x_ref, dy_ref, b_ref, c_ref, dt_ref, tl_ref, ex_ref, fade_ref, end_ref, gain_ref, pay_ref,
    ui_ref, dbi_ref, dci_ref, ri_ref,
    gs_ref, gt_ref, ga_ref, gb_ref, gc_ref, gk_ref,
    h_ref, g_ref, gains_ref, sel_ref, later_ref,
):
    k = pl.program_id(0)

    @pl.when(k == 0)
    def _():
        sel = selector()
        sel2 = twice(sel, 0)
        sel_ref[...] = sel2
        eye16 = iota((HEADS, HEADS), 0) == iota((HEADS, HEADS), 1)
        gains = jnp.sum(
            jnp.where(eye16, jnp.broadcast_to(gain_ref[...], (HEADS, HEADS)), 0.0),
            axis=1,
            keepdims=True,
        )
        gains_ref[...] = expand(jnp.broadcast_to(gains, (HEADS, 8)), sel2)
        ends = []
        sums = []
        for j in range(HEADS // 2):
            lanes = slice(128 * j, 128 * (j + 1))
            sums.append(pay_ref[2 * j, N + 1 : N + 2, :])
            total = jnp.zeros((8, 128), f32)
            for e in range(2):
                rows = slice(HALF * e, HALF * (e + 1))
                low_rows = slice(N + HALF * e, N + HALF * (e + 1))
                h = pay_ref[2 * j + e, 0:HALF, :]
                g = pay_ref[2 * j + e, HALF:N, :]
                h_ref[rows, lanes], h_ref[low_rows, lanes] = split(h)
                g_ref[rows, lanes], g_ref[low_rows, lanes] = split(g)
                end = (h.reshape(HALF // 8, 8, 128) * fade_ref[:, lanes][None]).reshape(HALF, 128)
                end = (end + end_ref[rows, lanes]) * g
                total = total + jnp.sum(end.reshape(HALF // 8, 8, 128), axis=0)
            ends.append(total)
        ends = jnp.concatenate(ends, axis=1)
        later = jnp.sum(dot(sel, split3(ends), 1, 1), axis=1, keepdims=True)
        later_ref[...] = jnp.broadcast_to(later, (HEADS, 128))
        sums = jnp.concatenate(sums, axis=0)
        low = low_half(sums.shape)
        even = jnp.sum(jnp.where(low, sums, 0.0), axis=1, keepdims=True)
        odd = jnp.sum(jnp.where(low, 0.0, sums), axis=1, keepdims=True)
        row, lane = iota((HEADS // 2, HEADS), 0), iota((HEADS // 2, HEADS), 1)
        skips = jnp.where(lane == 2 * row, even, jnp.where(lane == 2 * row + 1, odd, 0.0))
        gk_ref[...] = jnp.sum(skips, axis=0, keepdims=True)

    sel2 = sel_ref[...]
    sel = sel2[:HEADS]
    h2 = h_ref[...]
    g2 = g_ref[...]
    x = x_ref[...].astype(f32)
    dy = dy_ref[...].astype(f32)
    tails = dot(tl_ref[0], sel2, 0, 0)
    u = ui_ref[...] + tails * from_state(b_ref[...], g2)
    scaled = (dy.reshape(T // 8, 8, WIDE) * gains_ref[...][None]).reshape(T, WIDE)
    gs_ref[...] = (u + scaled).astype(bf16)
    cols = per_head(x * u, sel)
    gt_ref[...] = cols / dt_ref[...]
    gb_ref[...] = (dbi_ref[...] + to_maps(*split(x * tails), g2)).astype(bf16)
    ds = dy * dot(ex_ref[0], sel2, 0, 0)
    rows = ri_ref[...] + per_head(ds * from_state(c_ref[...], h2), sel)
    gc_ref[...] = (dci_ref[...] + to_maps(*split(ds), h2)).astype(bf16)
    after = times_ones(rows - cols, iota((T, T), 0) >= iota((T, T), 1)) + later_ref[:, 0:1]
    ga_ref[...] = after
    later_ref[...] = jnp.broadcast_to(after[:, 0:1], (HEADS, 128))


def last_part(
    signal, grad_out, keys, queries, steps, tails, expos, fade, end, gains, pay, u, db, dc, r
):
    length = signal.shape[0]
    last = length // T - 1
    tok = lambda width: pl.BlockSpec((T, width), lambda k: (last - k, 0))
    row = pl.BlockSpec((HEADS, T), lambda k: (0, last - k))
    scale = pl.BlockSpec((1, 2 * HEADS, T), lambda k: (last - k, 0, 0))
    return pl.pallas_call(
        last_kernel,
        grid=(length // T,),
        in_specs=[
            tok(WIDE), tok(WIDE), tok(N), tok(N), row, scale, scale, whole(fade.shape),
            whole(end.shape), whole(gains.shape), pl.BlockSpec(memory_space=pltpu.VMEM),
            tok(WIDE), tok(N), tok(N), row,
        ],
        out_specs=[tok(WIDE), row, row, tok(N), tok(N), whole((1, HEADS))],
        out_shape=[
            jax.ShapeDtypeStruct((length, WIDE), bf16),
            jax.ShapeDtypeStruct((HEADS, length), f32),
            jax.ShapeDtypeStruct((HEADS, length), f32),
            jax.ShapeDtypeStruct((length, N), bf16),
            jax.ShapeDtypeStruct((length, N), bf16),
            jax.ShapeDtypeStruct((1, HEADS), f32),
        ],
        scratch_shapes=[
            pltpu.VMEM((2 * N, WIDE), bf16),
            pltpu.VMEM((2 * N, WIDE), bf16),
            pltpu.VMEM((8, WIDE), f32),
            pltpu.VMEM((2 * HEADS, WIDE), bf16),
            pltpu.VMEM((HEADS, 128), f32),
        ],
        name="last_part",
    )(signal, grad_out, keys, queries, steps, tails, expos, fade, end, gains, pay, u, db, dc, r)


def on_device(signal, step_size, log_decay, input_map, output_map, skip_gain, grad_out):
    args = (signal, grad_out, input_map, output_map, step_size)
    pay, end, cums, fade, tails, expos = own_part(*args, log_decay)
    mine = lax.all_to_all(pay, "ctx", 0, 0, tiled=True)
    u, db, dc, r = first_part(*args, cums)
    mine, u = lax.optimization_barrier((mine, u))
    mine = pltpu.with_memory_space_constraint(mine, pltpu.VMEM)
    back = lax.all_to_all(scan_states(mine), "ctx", 0, 0, tiled=True)
    back = pltpu.with_memory_space_constraint(back, pltpu.VMEM)
    u, db, dc, r = second_part(*args, cums, u, db, dc, r)
    gs, gt, ga, gb, gc, gk = last_part(
        *args, tails, expos, fade, end, skip_gain.reshape(1, HEADS), back, u, db, dc, r
    )
    return gs, gt, ga, gb, gc, gk.reshape(HEADS)


def solution(mesh):
    placed = (
        P("ctx", "head"),
        P("head", "ctx"),
        P("head", "ctx"),
        P("ctx", "head"),
        P("ctx", "head"),
        P("head"),
        P("ctx", "head"),
    )
    return jax.shard_map(
        on_device,
        mesh=mesh,
        in_specs=placed,
        out_specs=(
            P("ctx", "head"),
            P("head", "ctx"),
            P("head", "ctx"),
            P("ctx", "head"),
            P("ctx", "head"),
            P("head"),
        ),
        check_vma=False,
    )
```

```python
import jax
import jax.numpy as jnp
from jax import lax
from jax.experimental import pallas as pl
from jax.experimental.pallas import tpu as pltpu
from jax.sharding import PartitionSpec as P

P_SIZE = 64
N = 128
HEADS = 16
Q = 128
T = 256
L = 256
HALF = N // 2
PAIRS = HEADS // 2
EARLY = 5
WIDE = HEADS * P_SIZE
ROWS = N + 8
LOG2E = 1.4426950408889634
NEG = -1e30
HIGH = lax.Precision.HIGHEST
f32 = jnp.float32
bf16 = jnp.bfloat16


def iota(shape, dim):
    return lax.broadcasted_iota(jnp.int32, shape, dim)


def split(z):
    hi = z.astype(bf16)
    lo = (z - hi.astype(f32)).astype(bf16)
    return hi, lo


def dot(a, b, ca, cb, precision=None):
    return lax.dot_general(
        a, b, (((ca,), (cb,)), ((), ())), precision=precision, preferred_element_type=f32
    )


def twice(a, axis):
    return jnp.concatenate([a, a], axis=axis)


def selector():
    return (iota((HEADS, WIDE), 1) // P_SIZE == iota((HEADS, WIDE), 0)).astype(f32).astype(bf16)


def paired(rows):
    return jnp.concatenate(split(rows), axis=0)


def expand(rows, sel2):
    return dot(paired(rows), sel2, 0, 0)


def per_head(z, sel):
    hi, lo = split(z)
    return dot(sel, hi, 1, 1) + dot(sel, lo, 1, 1)


def faded(state, fade):
    return (state.reshape(N // 8, 8, WIDE) * fade[None]).reshape(N, WIDE)


def folded(z):
    return jnp.sum(z.reshape(z.shape[0] // 8, 8, WIDE), axis=0)


def low_half(shape):
    return iota(shape, len(shape) - 1) < P_SIZE


def from_state(maps, state2):
    return dot(twice(maps, 1), state2, 1, 0)


def to_state(maps, hi, lo):
    return dot(twice(maps, 0), jnp.concatenate([hi, lo], axis=0), 0, 0)


def to_maps(hi, lo, state2):
    first = dot(hi, state2, 1, 1)
    return first[:, :N] + first[:, N:] + dot(lo, state2[:N], 1, 1)


def split3(z):
    hi = z.astype(bf16)
    rest = z - hi.astype(f32)
    mid = rest.astype(bf16)
    return jnp.concatenate([hi, mid, (rest - mid.astype(f32)).astype(bf16)], axis=0)


def times_ones(z, ones):
    out = dot(split3(z), ones.astype(f32).astype(bf16), 1, 0)
    size = z.shape[0]
    return out[:size] + out[size : 2 * size] + out[2 * size :]


def own_kernel(
    x_ref, dy_ref, b_ref, c_ref, dt_ref, a_ref,
    pay_ref, cum_ref, fade_ref, tl_ref, ex_ref, h_ref, p_ref, sk_ref, sel_ref,
):
    k = pl.program_id(0)
    count = a_ref.shape[1] // Q

    @pl.when(k == 0)
    def _():
        sk_ref[...] = jnp.zeros_like(sk_ref)
        h_ref[...] = jnp.zeros_like(h_ref)
        p_ref[...] = jnp.zeros_like(p_ref)
        sel = selector()
        sel_ref[...] = twice(sel, 0)
        stacked = jnp.concatenate([a_ref[:, Q * i : Q * (i + 1)] for i in range(count)], axis=0)
        sums = times_ones(stacked * LOG2E, iota((Q, Q), 0) <= iota((Q, Q), 1))
        run = jnp.zeros((HEADS, Q), f32)
        cums = []
        for i in range(count):
            cum = sums[HEADS * i : HEADS * (i + 1)]
            cum_ref[:, Q * i : Q * (i + 1)] = cum
            cums.append(cum + run)
            run = run + jnp.broadcast_to(cum[:, Q - 1 : Q], (HEADS, Q))
        fade_ref[...] = dot(split3(jnp.exp2(run[:, :8])), jnp.concatenate([sel] * 3, axis=0), 0, 0)
        for i in range(count):
            blk, off = (Q * i) // T, (Q * i) % T
            tails = jnp.exp2(run - cums[i]) * dt_ref[:, Q * i : Q * (i + 1)]
            tl_ref[blk, :, off : off + Q] = paired(tails)
            ex_ref[blk, :, off : off + Q] = paired(jnp.exp2(cums[i]))

    tails = tl_ref[k]
    expos = ex_ref[k]
    keys = b_ref[...]
    queries = c_ref[...]
    for i in range(WIDE // L):
        lanes = slice(L * i, L * (i + 1))
        sel2 = sel_ref[:, lanes]
        x = x_ref[:, lanes].astype(f32)
        h_ref[:, lanes] += to_state(keys, *split(x * dot(tails, sel2, 0, 0)))
        dy = dy_ref[:, lanes].astype(f32)
        p_ref[:, lanes] += to_state(queries, *split(dy * dot(expos, sel2, 0, 0)))
        sk_ref[:, lanes] += jnp.sum((x * dy).reshape(T // 8, 8, L), axis=0)

    @pl.when(k == pl.num_programs(0) - 1)
    def _():
        first = iota((8, 128), 0) == 0
        second = iota((8, 128), 0) == 1
        for j in range(HEADS // 2):
            lanes = slice(128 * j, 128 * (j + 1))
            skip = jnp.sum(sk_ref[:, lanes], axis=0, keepdims=True)
            tail = jnp.where(first, fade_ref[:, lanes], jnp.where(second, skip, 0.0))
            for e in range(2):
                rows = slice(HALF * e, HALF * (e + 1))
                pay_ref[2 * j + e, 0:HALF, :] = h_ref[rows, lanes]
                pay_ref[2 * j + e, HALF:N, :] = p_ref[rows, lanes]
                pay_ref[2 * j + e, N:ROWS, :] = tail


def whole(shape):
    return pl.BlockSpec(shape, lambda k: (0,) * len(shape))


def own_part(signal, grad_out, keys, queries, steps, decays):
    length = signal.shape[0]
    tok = lambda width: pl.BlockSpec((T, width), lambda k: (k, 0))
    outs = [
        ((HEADS, ROWS, 128), f32),
        ((HEADS, length), f32),
        ((8, WIDE), f32),
        ((length // T, 2 * HEADS, T), bf16),
        ((length // T, 2 * HEADS, T), bf16),
    ]
    return pl.pallas_call(
        own_kernel,
        grid=(length // T,),
        in_specs=[tok(WIDE), tok(WIDE), tok(N), tok(N), whole(steps.shape), whole(steps.shape)],
        out_specs=[whole(shape) for shape, _ in outs],
        out_shape=[jax.ShapeDtypeStruct(*o) for o in outs],
        scratch_shapes=[
            pltpu.VMEM((N, WIDE), f32),
            pltpu.VMEM((N, WIDE), f32),
            pltpu.VMEM((8, WIDE), f32),
            pltpu.VMEM((2 * HEADS, WIDE), bf16),
        ],
        name="own_part",
    )(signal, grad_out, keys, queries, steps, decays)


def scan_kernel(pay_ref, out_ref):
    count = pay_ref.shape[0]
    state = jnp.zeros((HALF, 128), f32)
    skip = jnp.zeros((8, 128), f32)
    for d in range(count):
        out_ref[d, 0:HALF, :] = state
        tail = pay_ref[d, N:ROWS, :]
        skip = skip + tail
        state = state * tail[0:1, :] + pay_ref[d, 0:HALF, :]
    state = jnp.zeros((HALF, 128), f32)
    for d in reversed(range(count)):
        out_ref[d, HALF:N, :] = state
        out_ref[d, N:ROWS, :] = skip
        state = state * pay_ref[d, N : N + 1, :] + pay_ref[d, HALF:N, :]


def scan_states(pay):
    return pl.pallas_call(
        scan_kernel,
        in_specs=[pl.BlockSpec(memory_space=pltpu.VMEM)],
        out_specs=pl.BlockSpec(memory_space=pltpu.VMEM),
        out_shape=jax.ShapeDtypeStruct(pay.shape, f32),
        name="scan_states",
    )(pay)


def inner_pairs(x_ref, dy_ref, keys, queries, cum, steps, pairs, r_ref):
    col = jnp.transpose(cum - jnp.log2(steps))
    scores = dot(keys, queries, 1, 1)
    mask = iota((Q, Q), 0) <= iota((Q, Q), 1)
    low = low_half((Q, 128))
    mixed = jnp.zeros((Q, Q), f32)
    us = []
    for j in pairs:
        lanes = slice(128 * j, 128 * (j + 1))
        dyp = dy_ref[:, lanes]
        zero = jnp.zeros_like(dyp)
        pair = jnp.concatenate([jnp.where(low, dyp, zero), jnp.where(low, zero, dyp)], axis=0)
        gram = dot(x_ref[:, lanes], pair, 1, 1)
        his, los = [], []
        for e in range(2):
            h = 2 * j + e
            g = gram[:, Q * e : Q * (e + 1)]
            decay = jnp.exp2(jnp.where(mask, cum[h : h + 1, :] - col[:, h : h + 1], NEG))
            weights = decay * scores
            mixed = mixed + decay * g
            r_ref[h : h + 1, :] += jnp.sum(weights * g, axis=0, keepdims=True)
            hi, lo = split(weights)
            his.append(hi)
            los.append(lo)
        both = jnp.concatenate(
            [jnp.concatenate(his, axis=1), jnp.concatenate(los, axis=1)], axis=0
        )
        out = dot(both, pair, 1, 0)
        us.append(out[:Q] + out[Q:])
    parts = paired(mixed)
    db = dot(parts, queries, 1, 0)
    return us, db[:Q] + db[Q:], dot(parts, twice(keys, 0), 0, 0)


def first_kernel(
    x_ref, dy_ref, b_ref, c_ref, dt_ref, cum_ref, u_ref, db_ref, dc_ref, r_ref, h_ref, sel_ref
):
    k = pl.program_id(0)

    @pl.when(k == 0)
    def _():
        h_ref[...] = jnp.zeros_like(h_ref)
        sel_ref[...] = twice(selector(), 0)

    cum = cum_ref[...]
    steps = dt_ref[...]
    keys = b_ref[...]
    queries = c_ref[...]
    sel2 = sel_ref[...]

    tot = jnp.broadcast_to(cum[:, Q - 1 : Q], (HEADS, Q))
    state = h_ref[...]
    state2 = paired(state)
    ds = dy_ref[...].astype(f32) * expand(jnp.exp2(cum), sel2)
    r_states = per_head(ds * from_state(queries, state2), sel2[:HEADS])
    dc_states = to_maps(*split(ds), state2)
    xs = x_ref[...].astype(f32) * expand(jnp.exp2(tot - cum) * steps, sel2)
    fade = expand(jnp.exp2(tot[:, :8]), sel2)
    h_ref[...] = faded(state, fade) + to_state(keys, *split(xs))

    r_ref[...] = r_states
    us, db, dc = inner_pairs(x_ref, dy_ref, keys, queries, cum, steps, range(EARLY), r_ref)
    for j, u in enumerate(us):
        u_ref[:, 128 * j : 128 * (j + 1)] = u
    db_ref[...] = db
    dc_ref[...] = dc_states + dc


def first_part(signal, grad_out, keys, queries, steps, cums):
    length = signal.shape[0]
    tok = lambda width: pl.BlockSpec((Q, width), lambda k: (k, 0))
    row = pl.BlockSpec((HEADS, Q), lambda k: (0, k))
    return pl.pallas_call(
        first_kernel,
        grid=(length // Q,),
        in_specs=[tok(WIDE), tok(WIDE), tok(N), tok(N), row, row],
        out_specs=[tok(WIDE), tok(N), tok(N), row, whole((N, WIDE))],
        out_shape=[
            jax.ShapeDtypeStruct((length, WIDE), f32),
            jax.ShapeDtypeStruct((length, N), f32),
            jax.ShapeDtypeStruct((length, N), f32),
            jax.ShapeDtypeStruct((HEADS, length), f32),
            jax.ShapeDtypeStruct((N, WIDE), f32),
        ],
        scratch_shapes=[pltpu.VMEM((2 * HEADS, WIDE), bf16)],
        name="first_part",
    )(signal, grad_out, keys, queries, steps, cums)


def second_kernel(
    x_ref, dy_ref, b_ref, c_ref, dt_ref, cum_ref, ui_ref, dbi_ref, dci_ref, ri_ref,
    u_ref, db_ref, dc_ref, r_ref, g_ref, sel_ref,
):
    k = pl.program_id(0)

    @pl.when(k == 0)
    def _():
        g_ref[...] = jnp.zeros_like(g_ref)
        sel_ref[...] = twice(selector(), 0)

    cum = cum_ref[...]
    steps = dt_ref[...]
    keys = b_ref[...]
    queries = c_ref[...]
    sel2 = sel_ref[...]
    tot = jnp.broadcast_to(cum[:, Q - 1 : Q], (HEADS, Q))
    state = g_ref[...]
    state2 = paired(state)
    tails = expand(jnp.exp2(tot - cum) * steps, sel2)
    passed = tails * from_state(keys, state2)
    db_states = to_maps(*split(x_ref[...].astype(f32) * tails), state2)
    ds = dy_ref[...].astype(f32) * expand(jnp.exp2(cum), sel2)
    fade = expand(jnp.exp2(tot[:, :8]), sel2)
    g_ref[...] = faded(state, fade) + to_state(queries, *split(ds))

    r_ref[...] = ri_ref[...]
    pairs = range(EARLY, PAIRS)
    us, db, dc = inner_pairs(x_ref, dy_ref, keys, queries, cum, steps, pairs, r_ref)
    done = 128 * EARLY
    u_ref[:, :done] = ui_ref[:, :done] + passed[:, :done]
    for j, u in zip(pairs, us):
        lanes = slice(128 * j, 128 * (j + 1))
        u_ref[:, lanes] = passed[:, lanes] + u
    db_ref[...] = dbi_ref[...] + db_states + db
    dc_ref[...] = dci_ref[...] + dc


def second_part(signal, grad_out, keys, queries, steps, cums, u, db, dc, r):
    length = signal.shape[0]
    last = length // Q - 1
    tok = lambda width: pl.BlockSpec((Q, width), lambda k: (last - k, 0))
    row = pl.BlockSpec((HEADS, Q), lambda k: (0, last - k))
    return pl.pallas_call(
        second_kernel,
        grid=(length // Q,),
        in_specs=[
            tok(WIDE), tok(WIDE), tok(N), tok(N), row, row, tok(WIDE), tok(N), tok(N), row,
        ],
        out_specs=[tok(WIDE), tok(N), tok(N), row],
        out_shape=[
            jax.ShapeDtypeStruct((length, WIDE), f32),
            jax.ShapeDtypeStruct((length, N), f32),
            jax.ShapeDtypeStruct((length, N), f32),
            jax.ShapeDtypeStruct((HEADS, length), f32),
        ],
        scratch_shapes=[pltpu.VMEM((N, WIDE), f32), pltpu.VMEM((2 * HEADS, WIDE), bf16)],
        name="second_part",
    )(signal, grad_out, keys, queries, steps, cums, u, db, dc, r)


def last_kernel(
    x_ref, dy_ref, b_ref, c_ref, dt_ref, tl_ref, ex_ref, fade_ref, end_ref, gain_ref, pay_ref,
    ui_ref, dbi_ref, dci_ref, ri_ref,
    gs_ref, gt_ref, ga_ref, gb_ref, gc_ref, gk_ref,
    h_ref, g_ref, gains_ref, sel_ref, later_ref,
):
    k = pl.program_id(0)

    @pl.when(k == 0)
    def _():
        sel = selector()
        sel2 = twice(sel, 0)
        sel_ref[...] = sel2
        eye16 = iota((HEADS, HEADS), 0) == iota((HEADS, HEADS), 1)
        gains = jnp.sum(
            jnp.where(eye16, jnp.broadcast_to(gain_ref[...], (HEADS, HEADS)), 0.0),
            axis=1,
            keepdims=True,
        )
        gains_ref[...] = expand(jnp.broadcast_to(gains, (HEADS, 8)), sel2)
        ends = []
        sums = []
        for j in range(HEADS // 2):
            lanes = slice(128 * j, 128 * (j + 1))
            sums.append(pay_ref[2 * j, N + 1 : N + 2, :])
            total = jnp.zeros((8, 128), f32)
            for e in range(2):
                rows = slice(HALF * e, HALF * (e + 1))
                low_rows = slice(N + HALF * e, N + HALF * (e + 1))
                h = pay_ref[2 * j + e, 0:HALF, :]
                g = pay_ref[2 * j + e, HALF:N, :]
                h_ref[rows, lanes], h_ref[low_rows, lanes] = split(h)
                g_ref[rows, lanes], g_ref[low_rows, lanes] = split(g)
                end = (h.reshape(HALF // 8, 8, 128) * fade_ref[:, lanes][None]).reshape(HALF, 128)
                end = (end + end_ref[rows, lanes]) * g
                total = total + jnp.sum(end.reshape(HALF // 8, 8, 128), axis=0)
            ends.append(total)
        ends = jnp.concatenate(ends, axis=1)
        later = jnp.sum(dot(sel, split3(ends), 1, 1), axis=1, keepdims=True)
        later_ref[...] = jnp.broadcast_to(later, (HEADS, 128))
        sums = jnp.concatenate(sums, axis=0)
        low = low_half(sums.shape)
        even = jnp.sum(jnp.where(low, sums, 0.0), axis=1, keepdims=True)
        odd = jnp.sum(jnp.where(low, 0.0, sums), axis=1, keepdims=True)
        row, lane = iota((HEADS // 2, HEADS), 0), iota((HEADS // 2, HEADS), 1)
        skips = jnp.where(lane == 2 * row, even, jnp.where(lane == 2 * row + 1, odd, 0.0))
        gk_ref[...] = jnp.sum(skips, axis=0, keepdims=True)

    sel2 = sel_ref[...]
    sel = sel2[:HEADS]
    h2 = h_ref[...]
    g2 = g_ref[...]
    x = x_ref[...].astype(f32)
    dy = dy_ref[...].astype(f32)
    tails = dot(tl_ref[0], sel2, 0, 0)
    u = ui_ref[...] + tails * from_state(b_ref[...], g2)
    scaled = (dy.reshape(T // 8, 8, WIDE) * gains_ref[...][None]).reshape(T, WIDE)
    gs_ref[...] = (u + scaled).astype(bf16)
    cols = per_head(x * u, sel)
    gt_ref[...] = cols / dt_ref[...]
    gb_ref[...] = (dbi_ref[...] + to_maps(*split(x * tails), g2)).astype(bf16)
    ds = dy * dot(ex_ref[0], sel2, 0, 0)
    rows = ri_ref[...] + per_head(ds * from_state(c_ref[...], h2), sel)
    gc_ref[...] = (dci_ref[...] + to_maps(*split(ds), h2)).astype(bf16)
    after = times_ones(rows - cols, iota((T, T), 0) >= iota((T, T), 1)) + later_ref[:, 0:1]
    ga_ref[...] = after
    later_ref[...] = jnp.broadcast_to(after[:, 0:1], (HEADS, 128))


def last_part(
    signal, grad_out, keys, queries, steps, tails, expos, fade, end, gains, pay, u, db, dc, r
):
    length = signal.shape[0]
    last = length // T - 1
    tok = lambda width: pl.BlockSpec((T, width), lambda k: (last - k, 0))
    row = pl.BlockSpec((HEADS, T), lambda k: (0, last - k))
    scale = pl.BlockSpec((1, 2 * HEADS, T), lambda k: (last - k, 0, 0))
    return pl.pallas_call(
        last_kernel,
        grid=(length // T,),
        in_specs=[
            tok(WIDE), tok(WIDE), tok(N), tok(N), row, scale, scale, whole(fade.shape),
            whole(end.shape), whole(gains.shape), pl.BlockSpec(memory_space=pltpu.VMEM),
            tok(WIDE), tok(N), tok(N), row,
        ],
        out_specs=[tok(WIDE), row, row, tok(N), tok(N), whole((1, HEADS))],
        out_shape=[
            jax.ShapeDtypeStruct((length, WIDE), bf16),
            jax.ShapeDtypeStruct((HEADS, length), f32),
            jax.ShapeDtypeStruct((HEADS, length), f32),
            jax.ShapeDtypeStruct((length, N), bf16),
            jax.ShapeDtypeStruct((length, N), bf16),
            jax.ShapeDtypeStruct((1, HEADS), f32),
        ],
        scratch_shapes=[
            pltpu.VMEM((2 * N, WIDE), bf16),
            pltpu.VMEM((2 * N, WIDE), bf16),
            pltpu.VMEM((8, WIDE), f32),
            pltpu.VMEM((2 * HEADS, WIDE), bf16),
            pltpu.VMEM((HEADS, 128), f32),
        ],
        name="last_part",
    )(signal, grad_out, keys, queries, steps, tails, expos, fade, end, gains, pay, u, db, dc, r)


def on_device(signal, step_size, log_decay, input_map, output_map, skip_gain, grad_out):
    args = (signal, grad_out, input_map, output_map, step_size)
    pay, cums, fade, tails, expos = own_part(*args, log_decay)
    mine = lax.all_to_all(pay, "ctx", 0, 0, tiled=True)
    u, db, dc, r, end = first_part(*args, cums)
    mine, u = lax.optimization_barrier((mine, u))
    mine = pltpu.with_memory_space_constraint(mine, pltpu.VMEM)
    back = lax.all_to_all(scan_states(mine), "ctx", 0, 0, tiled=True)
    back = pltpu.with_memory_space_constraint(back, pltpu.VMEM)
    u, db, dc, r = second_part(*args, cums, u, db, dc, r)
    gs, gt, ga, gb, gc, gk = last_part(
        *args, tails, expos, fade, end, skip_gain.reshape(1, HEADS), back, u, db, dc, r
    )
    return gs, gt, ga, gb, gc, gk.reshape(HEADS)


def solution(mesh):
    placed = (
        P("ctx", "head"),
        P("head", "ctx"),
        P("head", "ctx"),
        P("ctx", "head"),
        P("ctx", "head"),
        P("head"),
        P("ctx", "head"),
    )
    return jax.shard_map(
        on_device,
        mesh=mesh,
        in_specs=placed,
        out_specs=(
            P("ctx", "head"),
            P("head", "ctx"),
            P("head", "ctx"),
            P("ctx", "head"),
            P("ctx", "head"),
            P("head"),
        ),
        check_vma=False,
    )
```

```python
import jax
import jax.numpy as jnp
from jax import lax
from jax.experimental import pallas as pl
from jax.experimental.pallas import tpu as pltpu
from jax.sharding import PartitionSpec as P

P_SIZE = 64
N = 128
HEADS = 16
Q = 128
T = 256
L = 256
HALF = N // 2
PAIRS = HEADS // 2
EARLY = 5
WIDE = HEADS * P_SIZE
ROWS = N + 8
LOG2E = 1.4426950408889634
NEG = -1e30
HIGH = lax.Precision.HIGHEST
f32 = jnp.float32
bf16 = jnp.bfloat16


def iota(shape, dim):
    return lax.broadcasted_iota(jnp.int32, shape, dim)


def split(z):
    hi = z.astype(bf16)
    lo = (z - hi.astype(f32)).astype(bf16)
    return hi, lo


def dot(a, b, ca, cb, precision=None):
    return lax.dot_general(
        a, b, (((ca,), (cb,)), ((), ())), precision=precision, preferred_element_type=f32
    )


def twice(a, axis):
    return jnp.concatenate([a, a], axis=axis)


def selector():
    return (iota((HEADS, WIDE), 1) // P_SIZE == iota((HEADS, WIDE), 0)).astype(f32).astype(bf16)


def paired(rows):
    return jnp.concatenate(split(rows), axis=0)


def expand(rows, sel2):
    return dot(paired(rows), sel2, 0, 0)


def per_head(z, sel):
    hi, lo = split(z)
    return dot(sel, hi, 1, 1) + dot(sel, lo, 1, 1)


def faded(state, fade):
    return (state.reshape(N // 8, 8, WIDE) * fade[None]).reshape(N, WIDE)


def folded(z):
    return jnp.sum(z.reshape(z.shape[0] // 8, 8, WIDE), axis=0)


def low_half(shape):
    return iota(shape, len(shape) - 1) < P_SIZE


def from_state(maps, state2):
    return dot(twice(maps, 1), state2, 1, 0)


def to_state(maps, hi, lo):
    return dot(twice(maps, 0), jnp.concatenate([hi, lo], axis=0), 0, 0)


def to_maps(hi, lo, state2):
    first = dot(hi, state2, 1, 1)
    return first[:, :N] + first[:, N:] + dot(lo, state2[:N], 1, 1)


def split3(z):
    hi = z.astype(bf16)
    rest = z - hi.astype(f32)
    mid = rest.astype(bf16)
    return jnp.concatenate([hi, mid, (rest - mid.astype(f32)).astype(bf16)], axis=0)


def times_ones(z, ones):
    out = dot(split3(z), ones.astype(f32).astype(bf16), 1, 0)
    size = z.shape[0]
    return out[:size] + out[size : 2 * size] + out[2 * size :]


def own_kernel(
    x_ref, dy_ref, b_ref, c_ref, dt_ref, a_ref,
    pay_ref, cum_ref, fade_ref, tl_ref, ex_ref, h_ref, p_ref, sk_ref, sel_ref,
):
    k = pl.program_id(0)
    count = a_ref.shape[1] // Q

    @pl.when(k == 0)
    def _():
        sk_ref[...] = jnp.zeros_like(sk_ref)
        h_ref[...] = jnp.zeros_like(h_ref)
        p_ref[...] = jnp.zeros_like(p_ref)
        sel = selector()
        sel_ref[...] = twice(sel, 0)
        stacked = jnp.concatenate([a_ref[:, Q * i : Q * (i + 1)] for i in range(count)], axis=0)
        sums = times_ones(stacked * LOG2E, iota((Q, Q), 0) <= iota((Q, Q), 1))
        run = jnp.zeros((HEADS, Q), f32)
        cums = []
        for i in range(count):
            cum = sums[HEADS * i : HEADS * (i + 1)]
            cum_ref[:, Q * i : Q * (i + 1)] = cum
            cums.append(cum + run)
            run = run + jnp.broadcast_to(cum[:, Q - 1 : Q], (HEADS, Q))
        fade_ref[...] = dot(split3(jnp.exp2(run[:, :8])), jnp.concatenate([sel] * 3, axis=0), 0, 0)
        for i in range(count):
            blk, off = (Q * i) // T, (Q * i) % T
            tails = jnp.exp2(run - cums[i]) * dt_ref[:, Q * i : Q * (i + 1)]
            tl_ref[blk, :, off : off + Q] = paired(tails)
            ex_ref[blk, :, off : off + Q] = paired(jnp.exp2(cums[i]))

    tails = tl_ref[k]
    expos = ex_ref[k]
    keys = b_ref[...]
    queries = c_ref[...]
    for i in range(WIDE // L):
        lanes = slice(L * i, L * (i + 1))
        sel2 = sel_ref[:, lanes]
        x = x_ref[:, lanes].astype(f32)
        h_ref[:, lanes] += to_state(keys, *split(x * dot(tails, sel2, 0, 0)))
        dy = dy_ref[:, lanes].astype(f32)
        p_ref[:, lanes] += to_state(queries, *split(dy * dot(expos, sel2, 0, 0)))
        sk_ref[:, lanes] += jnp.sum((x * dy).reshape(T // 8, 8, L), axis=0)

    @pl.when(k == pl.num_programs(0) - 1)
    def _():
        first = iota((8, 128), 0) == 0
        second = iota((8, 128), 0) == 1
        for j in range(HEADS // 2):
            lanes = slice(128 * j, 128 * (j + 1))
            skip = jnp.sum(sk_ref[:, lanes], axis=0, keepdims=True)
            tail = jnp.where(first, fade_ref[:, lanes], jnp.where(second, skip, 0.0))
            for e in range(2):
                rows = slice(HALF * e, HALF * (e + 1))
                pay_ref[2 * j + e, 0:HALF, :] = h_ref[rows, lanes]
                pay_ref[2 * j + e, HALF:N, :] = p_ref[rows, lanes]
                pay_ref[2 * j + e, N:ROWS, :] = tail


def whole(shape):
    return pl.BlockSpec(shape, lambda k: (0,) * len(shape))


def own_part(signal, grad_out, keys, queries, steps, decays):
    length = signal.shape[0]
    tok = lambda width: pl.BlockSpec((T, width), lambda k: (k, 0))
    outs = [
        ((HEADS, ROWS, 128), f32),
        ((HEADS, length), f32),
        ((8, WIDE), f32),
        ((length // T, 2 * HEADS, T), bf16),
        ((length // T, 2 * HEADS, T), bf16),
    ]
    return pl.pallas_call(
        own_kernel,
        grid=(length // T,),
        in_specs=[tok(WIDE), tok(WIDE), tok(N), tok(N), whole(steps.shape), whole(steps.shape)],
        out_specs=[whole(shape) for shape, _ in outs],
        out_shape=[jax.ShapeDtypeStruct(*o) for o in outs],
        scratch_shapes=[
            pltpu.VMEM((N, WIDE), f32),
            pltpu.VMEM((N, WIDE), f32),
            pltpu.VMEM((8, WIDE), f32),
            pltpu.VMEM((2 * HEADS, WIDE), bf16),
        ],
        name="own_part",
    )(signal, grad_out, keys, queries, steps, decays)


def scan_kernel(pay_ref, out_ref):
    count = pay_ref.shape[0]
    state = jnp.zeros((HALF, 128), f32)
    skip = jnp.zeros((8, 128), f32)
    for d in range(count):
        out_ref[d, 0:HALF, :] = state
        tail = pay_ref[d, N:ROWS, :]
        skip = skip + tail
        state = state * tail[0:1, :] + pay_ref[d, 0:HALF, :]
    state = jnp.zeros((HALF, 128), f32)
    for d in reversed(range(count)):
        out_ref[d, HALF:N, :] = state
        out_ref[d, N:ROWS, :] = skip
        state = state * pay_ref[d, N : N + 1, :] + pay_ref[d, HALF:N, :]


def scan_states(pay):
    return pl.pallas_call(
        scan_kernel,
        in_specs=[pl.BlockSpec(memory_space=pltpu.VMEM)],
        out_specs=pl.BlockSpec(memory_space=pltpu.VMEM),
        out_shape=jax.ShapeDtypeStruct(pay.shape, f32),
        name="scan_states",
    )(pay)


def inner_pairs(x_ref, dy_ref, keys, queries, cum, steps, pairs, r_ref):
    col = jnp.transpose(cum - jnp.log2(steps))
    scores = dot(keys, queries, 1, 1)
    mask = iota((Q, Q), 0) <= iota((Q, Q), 1)
    low = low_half((Q, 128))
    mixed = jnp.zeros((Q, Q), f32)
    us = []
    for j in pairs:
        lanes = slice(128 * j, 128 * (j + 1))
        dyp = dy_ref[:, lanes]
        zero = jnp.zeros_like(dyp)
        pair = jnp.concatenate([jnp.where(low, dyp, zero), jnp.where(low, zero, dyp)], axis=0)
        gram = dot(x_ref[:, lanes], pair, 1, 1)
        his, los = [], []
        for e in range(2):
            h = 2 * j + e
            g = gram[:, Q * e : Q * (e + 1)]
            decay = jnp.exp2(jnp.where(mask, cum[h : h + 1, :] - col[:, h : h + 1], NEG))
            weights = decay * scores
            mixed = mixed + decay * g
            r_ref[h : h + 1, :] += jnp.sum(weights * g, axis=0, keepdims=True)
            hi, lo = split(weights)
            his.append(hi)
            los.append(lo)
        both = jnp.concatenate(
            [jnp.concatenate(his, axis=1), jnp.concatenate(los, axis=1)], axis=0
        )
        out = dot(both, pair, 1, 0)
        us.append(out[:Q] + out[Q:])
    parts = paired(mixed)
    db = dot(parts, queries, 1, 0)
    return us, db[:Q] + db[Q:], dot(parts, twice(keys, 0), 0, 0)


def first_kernel(
    x_ref, dy_ref, b_ref, c_ref, dt_ref, cum_ref, u_ref, db_ref, dc_ref, r_ref, h_ref, sel_ref
):
    k = pl.program_id(0)

    @pl.when(k == 0)
    def _():
        h_ref[...] = jnp.zeros_like(h_ref)
        sel_ref[...] = twice(selector(), 0)

    cum = cum_ref[...]
    steps = dt_ref[...]
    keys = b_ref[...]
    queries = c_ref[...]
    sel2 = sel_ref[...]

    tot = jnp.broadcast_to(cum[:, Q - 1 : Q], (HEADS, Q))
    state = h_ref[...]
    state2 = paired(state)
    ds = dy_ref[...].astype(f32) * expand(jnp.exp2(cum), sel2)
    r_states = per_head(ds * from_state(queries, state2), sel2[:HEADS])
    dc_states = to_maps(*split(ds), state2)
    xs = x_ref[...].astype(f32) * expand(jnp.exp2(tot - cum) * steps, sel2)
    fade = expand(jnp.exp2(tot[:, :8]), sel2)
    h_ref[...] = faded(state, fade) + to_state(keys, *split(xs))

    r_ref[...] = r_states
    us, db, dc = inner_pairs(x_ref, dy_ref, keys, queries, cum, steps, range(EARLY), r_ref)
    for j, u in enumerate(us):
        u_ref[:, 128 * j : 128 * (j + 1)] = u
    db_ref[...] = db
    dc_ref[...] = dc_states + dc


def first_part(signal, grad_out, keys, queries, steps, cums):
    length = signal.shape[0]
    tok = lambda width: pl.BlockSpec((Q, width), lambda k: (k, 0))
    row = pl.BlockSpec((HEADS, Q), lambda k: (0, k))
    return pl.pallas_call(
        first_kernel,
        grid=(length // Q,),
        in_specs=[tok(WIDE), tok(WIDE), tok(N), tok(N), row, row],
        out_specs=[tok(128 * EARLY), tok(N), tok(N), row, whole((N, WIDE))],
        out_shape=[
            jax.ShapeDtypeStruct((length, 128 * EARLY), f32),
            jax.ShapeDtypeStruct((length, N), f32),
            jax.ShapeDtypeStruct((length, N), f32),
            jax.ShapeDtypeStruct((HEADS, length), f32),
            jax.ShapeDtypeStruct((N, WIDE), f32),
        ],
        scratch_shapes=[pltpu.VMEM((2 * HEADS, WIDE), bf16)],
        name="first_part",
    )(signal, grad_out, keys, queries, steps, cums)


def second_kernel(
    x_ref, dy_ref, b_ref, c_ref, dt_ref, cum_ref, ui_ref, dbi_ref, dci_ref, ri_ref,
    u_ref, db_ref, dc_ref, r_ref, g_ref, sel_ref,
):
    k = pl.program_id(0)

    @pl.when(k == 0)
    def _():
        g_ref[...] = jnp.zeros_like(g_ref)
        sel_ref[...] = twice(selector(), 0)

    cum = cum_ref[...]
    steps = dt_ref[...]
    keys = b_ref[...]
    queries = c_ref[...]
    sel2 = sel_ref[...]
    tot = jnp.broadcast_to(cum[:, Q - 1 : Q], (HEADS, Q))
    state = g_ref[...]
    state2 = paired(state)
    tails = expand(jnp.exp2(tot - cum) * steps, sel2)
    passed = tails * from_state(keys, state2)
    db_states = to_maps(*split(x_ref[...].astype(f32) * tails), state2)
    ds = dy_ref[...].astype(f32) * expand(jnp.exp2(cum), sel2)
    fade = expand(jnp.exp2(tot[:, :8]), sel2)
    g_ref[...] = faded(state, fade) + to_state(queries, *split(ds))

    r_ref[...] = ri_ref[...]
    pairs = range(EARLY, PAIRS)
    us, db, dc = inner_pairs(x_ref, dy_ref, keys, queries, cum, steps, pairs, r_ref)
    done = 128 * EARLY
    u_ref[:, :done] = ui_ref[:, :done] + passed[:, :done]
    for j, u in zip(pairs, us):
        lanes = slice(128 * j, 128 * (j + 1))
        u_ref[:, lanes] = passed[:, lanes] + u
    db_ref[...] = dbi_ref[...] + db_states + db
    dc_ref[...] = dci_ref[...] + dc


def second_part(signal, grad_out, keys, queries, steps, cums, u, db, dc, r):
    length = signal.shape[0]
    last = length // Q - 1
    tok = lambda width: pl.BlockSpec((Q, width), lambda k: (last - k, 0))
    row = pl.BlockSpec((HEADS, Q), lambda k: (0, last - k))
    return pl.pallas_call(
        second_kernel,
        grid=(length // Q,),
        in_specs=[
            tok(WIDE), tok(WIDE), tok(N), tok(N), row, row, tok(128 * EARLY), tok(N), tok(N), row,
        ],
        out_specs=[tok(WIDE), tok(N), tok(N), row],
        out_shape=[
            jax.ShapeDtypeStruct((length, WIDE), f32),
            jax.ShapeDtypeStruct((length, N), f32),
            jax.ShapeDtypeStruct((length, N), f32),
            jax.ShapeDtypeStruct((HEADS, length), f32),
        ],
        scratch_shapes=[pltpu.VMEM((N, WIDE), f32), pltpu.VMEM((2 * HEADS, WIDE), bf16)],
        name="second_part",
    )(signal, grad_out, keys, queries, steps, cums, u, db, dc, r)


def last_kernel(
    x_ref, dy_ref, b_ref, c_ref, dt_ref, tl_ref, ex_ref, fade_ref, end_ref, gain_ref, pay_ref,
    ui_ref, dbi_ref, dci_ref, ri_ref,
    gs_ref, gt_ref, ga_ref, gb_ref, gc_ref, gk_ref,
    h_ref, g_ref, gains_ref, sel_ref, later_ref,
):
    k = pl.program_id(0)

    @pl.when(k == 0)
    def _():
        sel = selector()
        sel2 = twice(sel, 0)
        sel_ref[...] = sel2
        eye16 = iota((HEADS, HEADS), 0) == iota((HEADS, HEADS), 1)
        gains = jnp.sum(
            jnp.where(eye16, jnp.broadcast_to(gain_ref[...], (HEADS, HEADS)), 0.0),
            axis=1,
            keepdims=True,
        )
        gains_ref[...] = expand(jnp.broadcast_to(gains, (HEADS, 8)), sel2)
        ends = []
        sums = []
        for j in range(HEADS // 2):
            lanes = slice(128 * j, 128 * (j + 1))
            sums.append(pay_ref[2 * j, N + 1 : N + 2, :])
            total = jnp.zeros((8, 128), f32)
            for e in range(2):
                rows = slice(HALF * e, HALF * (e + 1))
                low_rows = slice(N + HALF * e, N + HALF * (e + 1))
                h = pay_ref[2 * j + e, 0:HALF, :]
                g = pay_ref[2 * j + e, HALF:N, :]
                h_ref[rows, lanes], h_ref[low_rows, lanes] = split(h)
                g_ref[rows, lanes], g_ref[low_rows, lanes] = split(g)
                end = (h.reshape(HALF // 8, 8, 128) * fade_ref[:, lanes][None]).reshape(HALF, 128)
                end = (end + end_ref[rows, lanes]) * g
                total = total + jnp.sum(end.reshape(HALF // 8, 8, 128), axis=0)
            ends.append(total)
        ends = jnp.concatenate(ends, axis=1)
        later = jnp.sum(dot(sel, split3(ends), 1, 1), axis=1, keepdims=True)
        later_ref[...] = jnp.broadcast_to(later, (HEADS, 128))
        sums = jnp.concatenate(sums, axis=0)
        low = low_half(sums.shape)
        even = jnp.sum(jnp.where(low, sums, 0.0), axis=1, keepdims=True)
        odd = jnp.sum(jnp.where(low, 0.0, sums), axis=1, keepdims=True)
        row, lane = iota((HEADS // 2, HEADS), 0), iota((HEADS // 2, HEADS), 1)
        skips = jnp.where(lane == 2 * row, even, jnp.where(lane == 2 * row + 1, odd, 0.0))
        gk_ref[...] = jnp.sum(skips, axis=0, keepdims=True)

    sel2 = sel_ref[...]
    sel = sel2[:HEADS]
    h2 = h_ref[...]
    g2 = g_ref[...]
    x = x_ref[...].astype(f32)
    dy = dy_ref[...].astype(f32)
    tails = dot(tl_ref[0], sel2, 0, 0)
    u = ui_ref[...] + tails * from_state(b_ref[...], g2)
    scaled = (dy.reshape(T // 8, 8, WIDE) * gains_ref[...][None]).reshape(T, WIDE)
    gs_ref[...] = (u + scaled).astype(bf16)
    cols = per_head(x * u, sel)
    gt_ref[...] = cols / dt_ref[...]
    gb_ref[...] = (dbi_ref[...] + to_maps(*split(x * tails), g2)).astype(bf16)
    ds = dy * dot(ex_ref[0], sel2, 0, 0)
    rows = ri_ref[...] + per_head(ds * from_state(c_ref[...], h2), sel)
    gc_ref[...] = (dci_ref[...] + to_maps(*split(ds), h2)).astype(bf16)
    after = times_ones(rows - cols, iota((T, T), 0) >= iota((T, T), 1)) + later_ref[:, 0:1]
    ga_ref[...] = after
    later_ref[...] = jnp.broadcast_to(after[:, 0:1], (HEADS, 128))


def last_part(
    signal, grad_out, keys, queries, steps, tails, expos, fade, end, gains, pay, u, db, dc, r
):
    length = signal.shape[0]
    last = length // T - 1
    tok = lambda width: pl.BlockSpec((T, width), lambda k: (last - k, 0))
    row = pl.BlockSpec((HEADS, T), lambda k: (0, last - k))
    scale = pl.BlockSpec((1, 2 * HEADS, T), lambda k: (last - k, 0, 0))
    return pl.pallas_call(
        last_kernel,
        grid=(length // T,),
        in_specs=[
            tok(WIDE), tok(WIDE), tok(N), tok(N), row, scale, scale, whole(fade.shape),
            whole(end.shape), whole(gains.shape), pl.BlockSpec(memory_space=pltpu.VMEM),
            tok(WIDE), tok(N), tok(N), row,
        ],
        out_specs=[tok(WIDE), row, row, tok(N), tok(N), whole((1, HEADS))],
        out_shape=[
            jax.ShapeDtypeStruct((length, WIDE), bf16),
            jax.ShapeDtypeStruct((HEADS, length), f32),
            jax.ShapeDtypeStruct((HEADS, length), f32),
            jax.ShapeDtypeStruct((length, N), bf16),
            jax.ShapeDtypeStruct((length, N), bf16),
            jax.ShapeDtypeStruct((1, HEADS), f32),
        ],
        scratch_shapes=[
            pltpu.VMEM((2 * N, WIDE), bf16),
            pltpu.VMEM((2 * N, WIDE), bf16),
            pltpu.VMEM((8, WIDE), f32),
            pltpu.VMEM((2 * HEADS, WIDE), bf16),
            pltpu.VMEM((HEADS, 128), f32),
        ],
        name="last_part",
    )(signal, grad_out, keys, queries, steps, tails, expos, fade, end, gains, pay, u, db, dc, r)


def on_device(signal, step_size, log_decay, input_map, output_map, skip_gain, grad_out):
    args = (signal, grad_out, input_map, output_map, step_size)
    pay, cums, fade, tails, expos = own_part(*args, log_decay)
    mine = lax.all_to_all(pay, "ctx", 0, 0, tiled=True)
    u, db, dc, r, end = first_part(*args, cums)
    mine, u = lax.optimization_barrier((mine, u))
    mine = pltpu.with_memory_space_constraint(mine, pltpu.VMEM)
    back = lax.all_to_all(scan_states(mine), "ctx", 0, 0, tiled=True)
    back = pltpu.with_memory_space_constraint(back, pltpu.VMEM)
    u, db, dc, r = second_part(*args, cums, u, db, dc, r)
    gs, gt, ga, gb, gc, gk = last_part(
        *args, tails, expos, fade, end, skip_gain.reshape(1, HEADS), back, u, db, dc, r
    )
    return gs, gt, ga, gb, gc, gk.reshape(HEADS)


def solution(mesh):
    placed = (
        P("ctx", "head"),
        P("head", "ctx"),
        P("head", "ctx"),
        P("ctx", "head"),
        P("ctx", "head"),
        P("head"),
        P("ctx", "head"),
    )
    return jax.shard_map(
        on_device,
        mesh=mesh,
        in_specs=placed,
        out_specs=(
            P("ctx", "head"),
            P("head", "ctx"),
            P("head", "ctx"),
            P("ctx", "head"),
            P("ctx", "head"),
            P("head"),
        ),
        check_vma=False,
    )
```
